32 devices in a mesh: group: 4 (over y, x), shard: 8 (over z, core).
Axes of the slice: x: 2, y: 2, z: 4, core: 2. Of those that a mesh axis runs over, the one named last changes fastest.
Arguments:
- queries: float32 [256, 768], P(('group', 'shard')), may hold values from -6 to 6
- codebook: float32 [96, 256, 8], replicated, may hold values from -0.21875 to 0.21875
- pq_codes: int32 [256, 96, 256], P(('group', 'shard')), may hold values from 0 to 255
- probes: int32 [256, 8], P('group'), may hold values from 0 to 63, all different within a row
- vectors: float32 [32768, 768], P(('group', 'shard')), may hold values from -0.21875 to 0.21875
- cand_owner: int32 [256, 16], P(('group', 'shard')), may hold values from 0 to 31, all different within a row; in each aligned block of 8 rows (0 to 7, 8 to 15, ...) at most 4 rows name the same one
- cand_row: int32 [256, 16], P(('group', 'shard')), may hold values from 0 to 1023
Outputs:
- pq_scores: float32 [256, 256, 64], P(('group', 'shard'))
- rerank_scores: float32 [256, 16], P(('group', 'shard'))
The draws below stay inside these ranges and needn't reach their ends.
Inputs may be any that keep to these rules, and one draw needn't show every extreme that they name: The 8 probes of one query are distinct. `cand_owner`: the 16 owners of one query are distinct. Among the queries of one device no owner appears more than 4 times, and some owner appears exactly 4 times.
All inputs are finite; a program needn't handle non-finite values.
Results may differ from the reference program's by a relative error of at most 0.0029.
Values may be sent and summed in bfloat16 or wider, within the bound.
No kernel may reach another device: no remote copies, remote signals or barrier semaphores. Data moves between devices by JAX's collectives and lax.ppermute only.
A program may use at most 128 MiB of HBM per device.

```python
import math
import jax
import jax.numpy as jnp
import numpy as np
from jax import lax

M = 96
DS = 8
D = 768
KS = 256
P_SIZE = 8
C = 16
LIST_LEN = 256
Q_DEV = 8
VEC_DEV = 1024
OWNERS = 32
GROUP_Q = 64
QUERIES = 256
LISTS_G = 64
LISTS = 256
VECS = 32768
CAP = 4


def plant(array, rng, low, high):
    longest = array.shape.index(max(array.shape))
    spots = []
    for shift in (0, 1):
        where = [jax.random.randint(jax.random.fold_in(rng, axis), (), 0, length) for axis, length in enumerate(array.shape)]
        where[longest] = (where[longest] + shift) % array.shape[longest]
        spots.append(tuple(where))
    return array.at[spots[0]].set(low).at[spots[1]].set(high)


def steps_of(key, extent, split, smallest, top_value):
    level, own = 1.0, jax.random.fold_in(key, 6)
    for axis_at, blocks in split:
        heights = jnp.exp(jax.random.uniform(jax.random.fold_in(own, axis_at), (blocks,), jnp.float32, smallest / len(split), top_value / len(split)))
        level = level * jnp.repeat(heights, extent[axis_at] // blocks).reshape([-1 if axis == axis_at else 1 for axis in range(len(extent))])
    return level


def distinct(key, rows, number_of, top, lift):
    sequence = jax.random.permutation(jax.random.fold_in(key, 1), number_of)
    favour = sequence
    for power in range(3):
        favour = favour * favour // number_of
    favour = favour * lift // number_of
    tickets = jax.random.randint(jax.random.fold_in(key, 2), (rows, number_of), 0, 4096) + favour
    holders = jax.random.permutation(jax.random.fold_in(key, 3), rows)[jnp.arange(number_of) % rows]
    tickets = jnp.where(jnp.arange(rows)[:, None] == holders[None, :], 1 << 14, tickets)
    merit = tickets * number_of + jnp.arange(number_of)
    return lax.top_k(merit.astype(jnp.int32), top)[1].astype(jnp.int32)


def assign_block(own_key, own, number, rows, number_of, top, bound, skew):
    order = jax.random.permutation(own_key, number_of)
    packed, ordinary = portions_of(number_of, rows * top, bound, skew, True), portions_of(number_of, rows * top, bound, skew, False)
    places = jnp.arange(number_of)

    def named(lengths, turn):
        used = int((lengths > 0).sum())
        fixed = max(1, used // 4)
        shifted = fixed + (places - fixed + turn * (used - fixed)) % max(1, number_of - fixed)
        return jnp.zeros((number_of,), jnp.int32).at[order[jnp.where(places < fixed, places, shifted)]].set(jnp.asarray(lengths, jnp.int32))

    lengths = jnp.where(number % 4 == 0, named(packed, number // 4), named(ordinary, number - number // 4 - 1))
    mixed = jax.random.permutation(jax.random.fold_in(own, 3), number_of)
    source_of, sink = mixed[0:number_of // 2 * 2:2], mixed[1:number_of // 2 * 2:2]
    margin = jnp.minimum(lengths[source_of] - 1, bound - lengths[sink]) // 2
    margin = jnp.where((source_of == order[0]) | (sink == order[0]) | (lengths[sink] == 0), 0, jnp.maximum(margin, 0))
    shifted = jax.random.randint(jax.random.fold_in(own, 4), (number_of // 2,), 0, 1 << 20) % (margin + 1)
    lengths = lengths.at[source_of].add(-shifted).at[sink].add(shifted)
    labels = jnp.searchsorted(jnp.cumsum(lengths), jnp.arange(rows * top), side="right").astype(jnp.int32)
    grid = labels.reshape(top, rows).T
    grid = grid[jax.random.permutation(jax.random.fold_in(own, 1), rows)]
    turn = jax.random.randint(jax.random.fold_in(own, 2), (rows, 1), 0, top)
    return jnp.take_along_axis(grid, (jnp.arange(top)[None, :] + turn) % top, axis=1)


def portions_of(number_of, total, limit, lean, full):
    loads = [(1 << 20) // math.isqrt(standing ** lean) + 1 for standing in range(1, number_of + 1)]
    largest = limit if full else min(limit, max(-(-total // number_of), total * loads[0] // sum(loads)))
    least = 1 if total - largest >= number_of - 1 else 0
    given, rest = [largest] + [least] * (number_of - 1), total - largest - least * (number_of - 1)
    while rest > 0:
        free = [i for i in range(1, number_of) if given[i] < largest] or [i for i in range(1, number_of) if given[i] < limit]
        pool, budget = sum([loads[i] for i in free]), rest
        for i in free:
            extra = min(limit - given[i], max(1, budget * loads[i] // pool), rest)
            given[i] = given[i] + extra
            rest = rest - extra
    return np.array(given)


def bell_draw(own_key, dims, spread, reach, split=(), kind=jnp.bfloat16):
    entries = jax.random.normal(own_key, dims, jnp.float32) * spread
    if len(split) > 0:
        entries = steps_of(own_key, dims, split, -0.22, 0.18) * entries
    return jnp.clip(entries, min=-reach, max=reach).astype(kind)


def setup_inputs(seed: int = 0) -> dict:
    streams_of = jax.random.split(jax.random.key(seed), 8)
    queries = bell_draw(streams_of[0], (QUERIES, D), 1.0, 6.0, ((0, 32),), jnp.float32)
    codebook = bell_draw(streams_of[1], (M, KS, DS), D ** -0.5, 0.21875, (), jnp.float32)
    pq_codes = plant(jax.random.randint(streams_of[2], (LISTS, M, LIST_LEN), 0, KS), jax.random.fold_in(streams_of[2], 1), 0, KS - 1).astype(jnp.int32)
    probes = distinct(streams_of[3], QUERIES, LISTS_G, P_SIZE, 2048)
    vectors = bell_draw(streams_of[4], (VECS, D), D ** -0.5, 0.21875, ((0, 32),), jnp.float32)
    cand_owner_keys = jax.random.split(jax.random.fold_in(streams_of[5], 1), QUERIES // Q_DEV)
    cand_owner_turns = jax.random.permutation(jax.random.fold_in(streams_of[5], 3), QUERIES // Q_DEV)
    cand_owner = jax.vmap(lambda own, number: assign_block(jax.random.fold_in(streams_of[5], 2), own, number, Q_DEV, OWNERS, C, CAP, 2))(cand_owner_keys, cand_owner_turns).reshape((QUERIES, C))
    cand_row = plant(jax.random.randint(streams_of[6], (QUERIES, C), 0, VEC_DEV), jax.random.fold_in(streams_of[6], 1), 0, VEC_DEV - 1).astype(jnp.int32)
    return {"queries": queries, "codebook": codebook, "pq_codes": pq_codes, "probes": probes, "vectors": vectors, "cand_owner": cand_owner, "cand_row": cand_row}


def reference(queries, codebook, pq_codes, probes, vectors, cand_owner, cand_row):
    number = queries.shape[0]
    tables = jnp.einsum("qmd,mkd->qmk", queries.reshape(number, M, DS), codebook, precision=lax.Precision.HIGHEST).astype(jnp.bfloat16)
    positions = jnp.arange(number, dtype=jnp.int32)
    group_of = positions // GROUP_Q
    within = positions % GROUP_Q
    chosen_lists = (probes + (group_of * LISTS_G)[:, None]).astype(jnp.int32)
    centre = jnp.arange(M, dtype=jnp.int32)

    def one_query(inputs):
        query_table, chosen = inputs
        picked = pq_codes[chosen]
        values = query_table[centre[None, :, None], picked].astype(jnp.float32)
        return jnp.sum(values, axis=1)

    totals = lax.map(one_query, (tables, chosen_lists))
    pq_scores = jnp.zeros((LISTS, LIST_LEN, GROUP_Q), jnp.float32)
    pq_scores = pq_scores.at[chosen_lists[:, :, None], jnp.arange(LIST_LEN, dtype=jnp.int32)[None, None, :], within[:, None, None]].set(totals)
    global_ids = (cand_owner * VEC_DEV + cand_row).astype(jnp.int32)
    found = vectors[global_ids]
    exact_scores = jnp.einsum("qd,qcd->qc", queries, found, precision=lax.Precision.HIGHEST)
    return pq_scores, exact_scores
```

```python
import jax
import jax.numpy as jnp
from jax import lax
from jax.experimental import pallas as pl
from jax.experimental.pallas import tpu as pltpu
from jax.sharding import PartitionSpec as P

AXES = ("group", "shard")
SUB = 8
LANE = 128
GATHER = lax.GatherDimensionNumbers(
    offset_dims=(),
    collapsed_slice_dims=(1,),
    start_index_map=(1,),
    operand_batching_dims=(0,),
    start_indices_batching_dims=(0,),
)


def pick(table, index):
    return lax.gather(
        table, index[..., None], GATHER, (1, 1), mode=lax.GatherScatterMode.PROMISE_IN_BOUNDS
    )


def pick_wide(table, index):
    low = jnp.bitwise_and(index, LANE - 1)
    result = pick(table[:, :LANE], low)
    for part in range(1, table.shape[1] // LANE):
        found = pick(table[:, part * LANE : (part + 1) * LANE], low)
        result = jnp.where(index >= part * LANE, found, result)
    return result


def split3(x):
    high = x.astype(jnp.bfloat16)
    rest = x - high.astype(jnp.float32)
    middle = rest.astype(jnp.bfloat16)
    low = (rest - middle.astype(jnp.float32)).astype(jnp.bfloat16)
    return high, middle, low


def owner_table(owner, row, owners):
    q_dev, cands = owner.shape
    width = -(-owners // LANE) * LANE
    lane = lax.broadcasted_iota(jnp.int32, (q_dev, width), 1)
    table = jnp.full((q_dev, width), -1, jnp.int32)
    for c in range(cands):
        table = jnp.where(lane == owner[:, c : c + 1], row[:, c : c + 1], table)
    return table


def before(table):
    asked = (table >= 0).astype(jnp.int32)
    rows = [jnp.zeros_like(asked[0:1])]
    for q in range(1, table.shape[0]):
        rows.append(rows[-1] + asked[q - 1 : q])
    return jnp.concatenate(rows, axis=0)


def layout_of(pair_count, owners, width):
    capacity = max(2, pair_count // owners)
    parts = max(
        p for p in range(1, 9) if p == 1 or (p * capacity <= SUB and width % (p * LANE) == 0)
    )
    slots = -(-capacity * parts // SUB) * SUB
    return capacity, parts, slots


def ids_kernel(capacity, parts, owner_ref, row_ref, out_ref):
    owners, slots = out_ref.shape[0], out_ref.shape[1]
    table = owner_table(owner_ref[...], row_ref[...], owners)
    rank = before(table)
    rows = []
    for s in range(capacity):
        rows.append(jnp.max(jnp.where(rank == s, table, -1), axis=0, keepdims=True))
    rows = rows * parts
    rows += [jnp.full_like(rows[0], -1)] * (slots - len(rows))
    packed = jnp.concatenate(rows, axis=0)
    for o in range(owners):
        out_ref[o] = jnp.broadcast_to(packed[:, o : o + 1], (slots, LANE))


def rows_kernel(capacity, parts, ids_ref, vectors_ref, out_ref):
    sources, slots = ids_ref.shape[0], ids_ref.shape[1]
    count, width = vectors_ref.shape
    piece = width // parts
    ids = ids_ref[...].reshape(sources * slots, LANE)
    pieces = []
    for block in range(count // LANE):
        lane = lax.broadcasted_iota(jnp.int32, (sources * slots, LANE), 1) + block * LANE
        pieces.append(jnp.where(ids == lane, 1.0, 0.0).astype(jnp.bfloat16))
    chosen = jnp.concatenate(pieces, axis=1)
    slot = lax.broadcasted_iota(jnp.int32, (sources * slots, piece), 0) % slots
    result = None
    for part in range(parts):
        vectors = vectors_ref[:, part * piece : (part + 1) * piece].astype(jnp.bfloat16)
        found = jnp.dot(chosen, vectors, preferred_element_type=jnp.float32)
        result = found if part == 0 else jnp.where(slot >= part * capacity, found, result)
    out_ref[...] = result.reshape(sources, slots, piece).astype(jnp.bfloat16)


def final_kernel(capacity, parts, owner_ref, row_ref, queries_ref, rows_ref, out_ref):
    owners, slots, piece = rows_ref.shape
    q_dev, cands = out_ref.shape
    rows = rows_ref[...].reshape(owners * slots, piece)
    total = None
    for part in range(parts):
        x = queries_ref[:, part * piece : (part + 1) * piece]
        stacked = jnp.concatenate(split3(x), axis=0)
        product = lax.dot_general(
            stacked, rows, (((1,), (1,)), ((), ())), preferred_element_type=jnp.float32
        )
        scores = product[:q_dev] + product[q_dev : 2 * q_dev] + product[2 * q_dev :]
        if part:
            width = scores.shape[1]
            scores = pltpu.roll(scores, width - part * capacity, axis=1)
        total = scores if part == 0 else total + scores
    owner = owner_ref[...]
    padded = jnp.concatenate([owner, jnp.zeros((q_dev, LANE - cands), jnp.int32)], axis=1)
    rank = before(owner_table(owner, row_ref[...], owners))
    place = padded * slots + pick_wide(rank, padded)
    out_ref[...] = pick_wide(total, place)[:, :cands]


def pq_kernel(
    q_dev, offsets, unroll, probes_ref, codebook_ref, codes_hbm, *refs
):
    number = len(offsets)
    chunk_refs, (out_ref, queries, table, codes, lists_v, lists_s, sems) = (
        refs[:number],
        refs[number:],
    )
    lists = codes.shape[0]
    subs, entries = codes.shape[1], codes.shape[2]
    total = queries.shape[0]
    centres = codebook_ref.shape[1]
    octets = subs // SUB
    shard = lax.axis_index("shard")
    load = pltpu.make_async_copy(codes_hbm, codes, sems.at[0])
    load.start()

    wanted = shard * lists + lax.broadcasted_iota(jnp.int32, (lists, total), 0)
    hit = jnp.zeros((lists, total), jnp.int32)
    for p in range(probes_ref.shape[0]):
        hit = jnp.where(probes_ref[p : p + 1, :] == wanted, 1, hit)
    upto = lax.broadcasted_iota(jnp.int32, (total, total), 0) >= lax.broadcasted_iota(
        jnp.int32, (total, total), 1
    )
    running = lax.dot_general(
        upto.astype(jnp.float32).astype(jnp.bfloat16),
        hit.astype(jnp.float32).astype(jnp.bfloat16),
        (((1,), (1,)), ((), ())),
        preferred_element_type=jnp.float32,
    )
    width = lists_v.shape[1]
    rank = lax.broadcasted_iota(jnp.int32, (total, width), 1).astype(jnp.float32)
    position = lax.broadcasted_iota(jnp.int32, (lists, total), 1)
    last = jnp.max(jnp.where(hit > 0, position, 0), axis=1, keepdims=True)
    counts = jnp.sum(hit, axis=1, keepdims=True)
    found = []
    for n in range(lists):
        passed = jnp.where(running[:, n : n + 1] <= rank, 1.0, 0.0)
        found.append(jnp.sum(passed, axis=0, keepdims=True))
    found = jnp.concatenate(found, axis=0).astype(jnp.int32)
    place = lax.broadcasted_iota(jnp.int32, (lists, width), 1)
    found = jnp.where(place < counts, found, last)
    found = jnp.where(place == width - 1, counts, found)
    lists_v[...] = found
    send = pltpu.make_async_copy(lists_v, lists_s, sems.at[1])
    send.start()

    for offset, ref in zip(offsets, chunk_refs):
        start = jnp.bitwise_xor(shard, offset) * q_dev if offset is not None else 0
        queries[pl.ds(pl.multiple_of(start, q_dev), ref.shape[0]), :] = ref[...]

    out_ref[...] = jnp.zeros(out_ref.shape, jnp.float32)

    half = LANE // 2
    lane = lax.broadcasted_iota(jnp.int32, (total, LANE), 1)
    inside = lax.broadcasted_iota(jnp.int32, (1, SUB, LANE), 2) % half // (half // SUB)
    own = jnp.where(inside == lax.broadcasted_iota(jnp.int32, (1, SUB, LANE), 1), 1.0, 0.0)

    def columns(k, carry):
        x = queries[:, pl.ds(pl.multiple_of(k * LANE, LANE), LANE)]
        swapped = pltpu.roll(x, half, axis=1)
        for side in range(2):
            wide = jnp.where((lane < half) == (side == 0), x, swapped)
            high = wide.astype(jnp.bfloat16).astype(jnp.float32)
            terms = []
            for term in (high, wide - high):
                spread = (term[:, None, :] * own).reshape(total * SUB, LANE)
                terms.append(spread.astype(jnp.bfloat16))
            c = codebook_ref[pl.ds(pl.multiple_of(k * LANE + side * half, half), half), :]
            c_high = c.astype(jnp.bfloat16)
            c_low = (c - c_high.astype(jnp.float32)).astype(jnp.bfloat16)
            weights = jnp.concatenate([c_high, c_low, c_high, c_low], axis=0)
            product = jnp.dot(
                jnp.concatenate(terms, axis=1), weights, preferred_element_type=jnp.float32
            )
            table[:, 2 * k + side] = product.reshape(total, SUB, centres)
        return carry

    lax.fori_loop(0, octets // 2, columns, 0)
    load.wait()
    send.wait()

    def one_list(n, carry):
        count = lists_s[n, width - 1]

        def some(step, inner):
            chosen = [lists_s[n, step * unroll + u] for u in range(unroll)]
            sums = [[None] * (entries // LANE) for _ in range(unroll)]
            for i in range(octets):
                for h in range(entries // LANE):
                    code = codes[n, i * SUB : (i + 1) * SUB, h * LANE : (h + 1) * LANE]
                    low = jnp.bitwise_and(code, LANE - 1)
                    for u in range(unroll):
                        value = pick(table[chosen[u], i, :, 0:LANE], low)
                        for part in range(1, centres // LANE):
                            other = pick(
                                table[chosen[u], i, :, part * LANE : (part + 1) * LANE], low
                            )
                            value = jnp.where(code >= part * LANE, other, value)
                        sums[u][h] = value if i == 0 else sums[u][h] + value
            for u in range(unroll):
                line = [jnp.sum(s, axis=0, keepdims=True) for s in sums[u]]
                out_ref[n, pl.ds(chosen[u], 1), :] = jnp.concatenate(line, axis=1)
            return inner

        return lax.fori_loop(0, (count + unroll - 1) // unroll, some, carry)

    lax.fori_loop(0, lists, one_list, 0)


def whole(memory=pltpu.VMEM):
    return pl.BlockSpec(memory_space=memory)


def per_device(queries, codebook, pq_codes, probes, vectors, cand_owner, cand_row):
    shards = lax.axis_size("shard")
    owners = lax.axis_size("group") * shards
    q_dev, width = queries.shape
    cands = cand_owner.shape[1]
    subs, centres, dims = codebook.shape
    lists, _, entries = pq_codes.shape
    total = q_dev * shards
    capacity, parts, slots = layout_of(q_dev * cands, owners, width)
    unroll = 4

    ids = pl.pallas_call(
        lambda *refs: ids_kernel(capacity, parts, *refs),
        out_shape=jax.ShapeDtypeStruct((owners, slots, LANE), jnp.int32),
        in_specs=[whole()] * 2,
        out_specs=whole(),
        name="ids",
    )(cand_owner, cand_row)
    asked = lax.all_to_all(ids, AXES, split_axis=0, concat_axis=0, tiled=True)

    if shards == 8:
        offsets = tuple(range(shards))
        chunks = [queries] + [
            lax.ppermute(queries, "shard", [(i, i ^ k) for i in range(shards)])
            for k in range(1, shards)
        ]
    else:
        offsets = (None,)
        chunks = [lax.all_gather(queries, "shard", axis=0, tiled=True)]

    rows = pl.pallas_call(
        lambda *refs: rows_kernel(capacity, parts, *refs),
        out_shape=jax.ShapeDtypeStruct((owners, slots, width // parts), jnp.bfloat16),
        in_specs=[whole()] * 2,
        out_specs=whole(),
        name="rows",
        compiler_params=pltpu.CompilerParams(vmem_limit_bytes=24 << 20),
        cost_estimate=pl.CostEstimate(flops=10**9, bytes_accessed=4 << 20, transcendentals=0),
    )(asked, vectors)
    returned = lax.all_to_all(rows, AXES, split_axis=0, concat_axis=0, tiled=True)

    list_width = -(-(total + unroll + 1) // LANE) * LANE
    pq = pl.pallas_call(
        lambda *refs: pq_kernel(q_dev, offsets, unroll, *refs),
        out_shape=jax.ShapeDtypeStruct((lists, total, entries), jnp.float32),
        in_specs=[whole(), whole(), whole(pl.ANY)] + [whole()] * len(chunks),
        out_specs=whole(),
        scratch_shapes=[
            pltpu.VMEM((total, width), jnp.float32),
            pltpu.VMEM((total, subs // SUB, SUB, centres), jnp.float32),
            pltpu.VMEM((lists, subs, entries), jnp.int32),
            pltpu.VMEM((lists, list_width), jnp.int32),
            pltpu.SMEM((lists, list_width), jnp.int32),
            pltpu.SemaphoreType.DMA((2,)),
        ],
        name="pq",
        compiler_params=pltpu.CompilerParams(vmem_limit_bytes=40 << 20),
        cost_estimate=pl.CostEstimate(
            flops=10**10, bytes_accessed=30 << 20, transcendentals=0
        ),
    )(
        probes.T,
        codebook.transpose(0, 2, 1).reshape(subs * dims, centres),
        pq_codes,
        *chunks,
    )

    rerank = pl.pallas_call(
        lambda *refs: final_kernel(capacity, parts, *refs),
        out_shape=jax.ShapeDtypeStruct((q_dev, cands), jnp.float32),
        in_specs=[whole()] * 4,
        out_specs=whole(),
        name="final",
    )(cand_owner, cand_row, queries, returned)
    return pq.transpose(0, 2, 1), rerank


def solution(mesh):
    in_specs = (
        P(AXES, None),
        P(),
        P(AXES, None, None),
        P("group", None),
        P(AXES, None),
        P(AXES, None),
        P(AXES, None),
    )
    out_specs = (P(AXES, None, None), P(AXES, None))
    return jax.shard_map(
        per_device, mesh=mesh, in_specs=in_specs, out_specs=out_specs, check_vma=False
    )
```

```python
import jax
import jax.numpy as jnp
from jax import lax
from jax.experimental import pallas as pl
from jax.experimental.pallas import tpu as pltpu
from jax.sharding import PartitionSpec as P

AXES = ("group", "shard")
SUB = 8
LANE = 128
GATHER = lax.GatherDimensionNumbers(
    offset_dims=(),
    collapsed_slice_dims=(1,),
    start_index_map=(1,),
    operand_batching_dims=(0,),
    start_indices_batching_dims=(0,),
)


def pick(table, index):
    return lax.gather(
        table, index[..., None], GATHER, (1, 1), mode=lax.GatherScatterMode.PROMISE_IN_BOUNDS
    )


def pick_wide(table, index):
    low = jnp.bitwise_and(index, LANE - 1)
    result = pick(table[:, :LANE], low)
    for part in range(1, table.shape[1] // LANE):
        found = pick(table[:, part * LANE : (part + 1) * LANE], low)
        result = jnp.where(index >= part * LANE, found, result)
    return result


def split3(x):
    high = x.astype(jnp.bfloat16)
    rest = x - high.astype(jnp.float32)
    middle = rest.astype(jnp.bfloat16)
    low = (rest - middle.astype(jnp.float32)).astype(jnp.bfloat16)
    return high, middle, low


def owner_table(owner, row, owners):
    q_dev, cands = owner.shape
    width = -(-owners // LANE) * LANE
    lane = lax.broadcasted_iota(jnp.int32, (q_dev, width), 1)
    table = jnp.full((q_dev, width), -1, jnp.int32)
    for c in range(cands):
        table = jnp.where(lane == owner[:, c : c + 1], row[:, c : c + 1], table)
    return table


def before(table):
    asked = (table >= 0).astype(jnp.int32)
    rows = [jnp.zeros_like(asked[0:1])]
    for q in range(1, table.shape[0]):
        rows.append(rows[-1] + asked[q - 1 : q])
    return jnp.concatenate(rows, axis=0)


def layout_of(pair_count, owners, width):
    capacity = max(2, pair_count // owners)
    parts = max(
        p for p in range(1, 9) if p == 1 or (p * capacity <= SUB and width % (p * LANE) == 0)
    )
    slots = -(-capacity * parts // SUB) * SUB
    return capacity, parts, slots


def ids_kernel(capacity, parts, owner_ref, row_ref, out_ref):
    owners, slots = out_ref.shape[0], out_ref.shape[1]
    table = owner_table(owner_ref[...], row_ref[...], owners)
    rank = before(table)
    rows = []
    for s in range(capacity):
        rows.append(jnp.max(jnp.where(rank == s, table, -1), axis=0, keepdims=True))
    rows = rows * parts
    rows += [jnp.full_like(rows[0], -1)] * (slots - len(rows))
    packed = jnp.concatenate(rows, axis=0)
    for o in range(owners):
        out_ref[o] = jnp.broadcast_to(packed[:, o : o + 1], (slots, LANE))


def rows_kernel(capacity, parts, ids_ref, vectors_ref, out_ref):
    sources, slots = ids_ref.shape[0], ids_ref.shape[1]
    count, width = vectors_ref.shape
    piece = width // parts
    ids = ids_ref[...].reshape(sources * slots, LANE)
    pieces = []
    for block in range(count // LANE):
        lane = lax.broadcasted_iota(jnp.int32, (sources * slots, LANE), 1) + block * LANE
        pieces.append(jnp.where(ids == lane, 1.0, 0.0).astype(jnp.bfloat16))
    chosen = jnp.concatenate(pieces, axis=1)
    slot = lax.broadcasted_iota(jnp.int32, (sources * slots, piece), 0) % slots
    result = None
    for part in range(parts):
        vectors = vectors_ref[:, part * piece : (part + 1) * piece]
        found = jnp.dot(chosen, vectors, preferred_element_type=jnp.float32)
        result = found if part == 0 else jnp.where(slot >= part * capacity, found, result)
    out_ref[...] = result.reshape(sources, slots, piece).astype(jnp.bfloat16)


def final_kernel(capacity, parts, owner_ref, row_ref, queries_ref, rows_ref, out_ref):
    owners, slots, piece = rows_ref.shape
    q_dev, cands = out_ref.shape
    rows = rows_ref[...].reshape(owners * slots, piece)
    total = None
    for part in range(parts):
        x = queries_ref[:, part * piece : (part + 1) * piece]
        stacked = jnp.concatenate(split3(x), axis=0)
        product = lax.dot_general(
            stacked, rows, (((1,), (1,)), ((), ())), preferred_element_type=jnp.float32
        )
        scores = product[:q_dev] + product[q_dev : 2 * q_dev] + product[2 * q_dev :]
        if part:
            width = scores.shape[1]
            scores = pltpu.roll(scores, width - part * capacity, axis=1)
        total = scores if part == 0 else total + scores
    owner = owner_ref[...]
    padded = jnp.concatenate([owner, jnp.zeros((q_dev, LANE - cands), jnp.int32)], axis=1)
    rank = before(owner_table(owner, row_ref[...], owners))
    place = padded * slots + pick_wide(rank, padded)
    out_ref[...] = pick_wide(total, place)[:, :cands]


def pq_kernel(q_dev, pieces, unroll, probes_ref, codebook_ref, codes_ref, *refs):
    number = len(pieces)
    chunk_refs, (out_ref, queries, table, codes, lists_v, lists_s, sem) = (
        refs[:number],
        refs[number:],
    )
    lists, subs, entries = codes.shape
    total = queries.shape[0]
    centres = codebook_ref.shape[1]
    rows = 2 * SUB
    blocks = subs // rows
    shard = lax.axis_index("shard")

    wanted = shard * lists + lax.broadcasted_iota(jnp.int32, (lists, total), 0)
    hit = jnp.zeros((lists, total), jnp.int32)
    for p in range(probes_ref.shape[0]):
        hit = jnp.where(probes_ref[p : p + 1, :] == wanted, 1, hit)
    upto = lax.broadcasted_iota(jnp.int32, (total, total), 0) >= lax.broadcasted_iota(
        jnp.int32, (total, total), 1
    )
    running = lax.dot_general(
        upto.astype(jnp.float32).astype(jnp.bfloat16),
        hit.astype(jnp.float32).astype(jnp.bfloat16),
        (((1,), (1,)), ((), ())),
        preferred_element_type=jnp.float32,
    )
    width = lists_v.shape[1]
    rank = lax.broadcasted_iota(jnp.int32, (total, width), 1).astype(jnp.float32)
    position = lax.broadcasted_iota(jnp.int32, (lists, total), 1)
    last = jnp.max(jnp.where(hit > 0, position, 0), axis=1, keepdims=True)
    counts = jnp.sum(hit, axis=1, keepdims=True)
    found = []
    for n in range(lists):
        passed = jnp.where(running[:, n : n + 1] <= rank, 1.0, 0.0)
        found.append(jnp.sum(passed, axis=0, keepdims=True))
    found = jnp.concatenate(found, axis=0).astype(jnp.int32)
    place = lax.broadcasted_iota(jnp.int32, (lists, width), 1)
    found = jnp.where(place < counts, found, last)
    found = jnp.where(place == width - 1, counts, found)
    lists_v[...] = found
    send = pltpu.make_async_copy(lists_v, lists_s, sem)
    send.start()

    for (offset, begin, size), ref in zip(pieces, chunk_refs):
        start = 0 if offset is None else jnp.bitwise_xor(shard, offset) * q_dev
        queries[pl.ds(pl.multiple_of(start, q_dev), size), :] = ref[begin : begin + size, :]

    out_ref[...] = jnp.zeros(out_ref.shape, jnp.float32)
    for n in range(lists):
        codes[n] = codes_ref[n].astype(jnp.int16)

    half = LANE // 2
    lane = lax.broadcasted_iota(jnp.int32, (total, LANE), 1)
    inside = lax.broadcasted_iota(jnp.int32, (1, SUB, LANE), 2) % half // (half // SUB)
    own = jnp.where(inside == lax.broadcasted_iota(jnp.int32, (1, SUB, LANE), 1), 1.0, 0.0)

    def columns(k, carry):
        x = queries[:, pl.ds(pl.multiple_of(k * LANE, LANE), LANE)]
        swapped = pltpu.roll(x, half, axis=1)
        products = []
        for side in range(2):
            wide = jnp.where((lane < half) == (side == 0), x, swapped)
            high = wide.astype(jnp.bfloat16).astype(jnp.float32)
            terms = []
            for term in (high, wide - high):
                spread = (term[:, None, :] * own).reshape(total * SUB, LANE)
                terms.append(spread.astype(jnp.bfloat16))
            c = codebook_ref[pl.ds(pl.multiple_of(k * LANE + side * half, half), half), :]
            c_high = c.astype(jnp.bfloat16)
            c_low = (c - c_high.astype(jnp.float32)).astype(jnp.bfloat16)
            weights = jnp.concatenate([c_high, c_low, c_high, c_low], axis=0)
            product = jnp.dot(
                jnp.concatenate(terms, axis=1), weights, preferred_element_type=jnp.float32
            )
            products.append(product.reshape(total, SUB, centres))
        table[:, k] = jnp.concatenate(products, axis=1).astype(jnp.bfloat16)
        return carry

    lax.fori_loop(0, blocks, columns, 0)
    send.wait()
    halves = entries // LANE

    def emit(n, chosen, sums):
        for u in range(unroll):
            line = [
                jnp.sum(s, axis=0, keepdims=True) for s in sums[u * halves : (u + 1) * halves]
            ]
            out_ref[n, pl.ds(chosen[u], 1), :] = jnp.concatenate(line, axis=1)

    def one_list(n, carry):
        count = lists_s[n, width - 1]

        def some(step, inner):
            chosen = tuple(lists_s[n, step * unroll + u] for u in range(unroll))
            sums = [None] * (unroll * halves)
            for i in range(blocks):
                for h in range(halves):
                    code = codes[n, i * rows : (i + 1) * rows, h * LANE : (h + 1) * LANE]
                    low = jnp.bitwise_and(code, jnp.int16(LANE - 1))
                    for u in range(unroll):
                        value = pick(table[chosen[u], i, :, 0:LANE], low)
                        for part in range(1, centres // LANE):
                            other = pick(
                                table[chosen[u], i, :, part * LANE : (part + 1) * LANE], low
                            )
                            value = jnp.where(code >= jnp.int16(part * LANE), other, value)
                        value = value.astype(jnp.float32)
                        value = value[:SUB] + value[SUB:]
                        at = u * halves + h
                        sums[at] = value if i == 0 else sums[at] + value
                if i == 1:
                    emit(*inner)
            return n, chosen, tuple(sums)

        return lax.fori_loop(0, (count + unroll - 1) // unroll, some, carry)

    first = (
        jnp.int32(0),
        (jnp.int32(0),) * unroll,
        (jnp.zeros((SUB, LANE), jnp.float32),) * (unroll * halves),
    )
    emit(*lax.fori_loop(0, lists, one_list, first))


def whole(memory=pltpu.VMEM):
    return pl.BlockSpec(memory_space=memory)


def per_device(queries, codebook, pq_codes, probes, vectors, cand_owner, cand_row):
    shards = lax.axis_size("shard")
    owners = lax.axis_size("group") * shards
    q_dev, width = queries.shape
    cands = cand_owner.shape[1]
    subs, centres, dims = codebook.shape
    lists, _, entries = pq_codes.shape
    total = q_dev * shards
    capacity, parts, slots = layout_of(q_dev * cands, owners, width)
    unroll = 8

    ids = pl.pallas_call(
        lambda *refs: ids_kernel(capacity, parts, *refs),
        out_shape=jax.ShapeDtypeStruct((owners, slots, LANE), jnp.int32),
        in_specs=[whole()] * 2,
        out_specs=whole(),
        name="ids",
    )(cand_owner, cand_row)
    asked = lax.all_to_all(ids, AXES, split_axis=0, concat_axis=0, tiled=True)

    pieces, chunks = [], []
    if shards == 8:
        partner = lax.ppermute(queries, "shard", [(i, i ^ 1) for i in range(shards)])
        pair = jnp.concatenate([queries, partner], axis=0)
        for k in range(0, shards, 2):
            chunk = pair
            if k:
                chunk = lax.ppermute(pair, "shard", [(i, i ^ k) for i in range(shards)])
            chunks += [chunk, chunk]
            pieces += [(k, 0, q_dev), (k ^ 1, q_dev, q_dev)]
    else:
        pieces.append((None, 0, total))
        chunks.append(lax.all_gather(queries, "shard", axis=0, tiled=True))

    rows = pl.pallas_call(
        lambda *refs: rows_kernel(capacity, parts, *refs),
        out_shape=jax.ShapeDtypeStruct((owners, slots, width // parts), jnp.bfloat16),
        in_specs=[whole()] * 2,
        out_specs=whole(),
        name="rows",
        compiler_params=pltpu.CompilerParams(vmem_limit_bytes=16 << 20),
        cost_estimate=pl.CostEstimate(flops=10**9, bytes_accessed=4 << 20, transcendentals=0),
    )(asked, vectors.astype(jnp.bfloat16))
    returned = lax.all_to_all(rows, AXES, split_axis=0, concat_axis=0, tiled=True)

    list_width = -(-(total + unroll + 1) // LANE) * LANE
    pq = pl.pallas_call(
        lambda *refs: pq_kernel(q_dev, pieces, unroll, *refs),
        out_shape=jax.ShapeDtypeStruct((lists, total, entries), jnp.float32),
        in_specs=[whole()] * (3 + len(chunks)),
        out_specs=whole(),
        scratch_shapes=[
            pltpu.VMEM((total, width), jnp.float32),
            pltpu.VMEM((total, subs // SUB // 2, 2 * SUB, centres), jnp.bfloat16),
            pltpu.VMEM((lists, subs, entries), jnp.int16),
            pltpu.VMEM((lists, list_width), jnp.int32),
            pltpu.SMEM((lists, list_width), jnp.int32),
            pltpu.SemaphoreType.DMA,
        ],
        name="pq",
        compiler_params=pltpu.CompilerParams(
            vmem_limit_bytes=(8 << 20) + 4 * total * subs * centres
        ),
        cost_estimate=pl.CostEstimate(
            flops=10**10, bytes_accessed=30 << 20, transcendentals=0
        ),
    )(
        probes.T,
        codebook.transpose(0, 2, 1).reshape(subs * dims, centres),
        pq_codes,
        *chunks,
    )

    rerank = pl.pallas_call(
        lambda *refs: final_kernel(capacity, parts, *refs),
        out_shape=jax.ShapeDtypeStruct((q_dev, cands), jnp.float32),
        in_specs=[whole()] * 4,
        out_specs=whole(),
        name="final",
        compiler_params=pltpu.CompilerParams(vmem_limit_bytes=8 << 20),
    )(cand_owner, cand_row, queries, returned)
    return pq.transpose(0, 2, 1), rerank


def solution(mesh):
    in_specs = (
        P(AXES, None),
        P(),
        P(AXES, None, None),
        P("group", None),
        P(AXES, None),
        P(AXES, None),
        P(AXES, None),
    )
    out_specs = (P(AXES, None, None), P(AXES, None))
    return jax.shard_map(
        per_device, mesh=mesh, in_specs=in_specs, out_specs=out_specs, check_vma=False
    )
```

```python
import jax
import jax.numpy as jnp
from jax import lax
from jax.experimental import pallas as pl
from jax.experimental.pallas import tpu as pltpu
from jax.sharding import PartitionSpec as P


AXES = ("group", "shard")
SUB = 8
LANE = 128
GATHER = lax.GatherDimensionNumbers(
    offset_dims=(),
    collapsed_slice_dims=(1,),
    start_index_map=(1,),
    operand_batching_dims=(0,),
    start_indices_batching_dims=(0,),
)


def pick(table, index):
    return lax.gather(
        table, index[..., None], GATHER, (1, 1), mode=lax.GatherScatterMode.PROMISE_IN_BOUNDS
    )


def pick_wide(table, index):
    low = jnp.bitwise_and(index, LANE - 1)
    result = pick(table[:, :LANE], low)
    for part in range(1, table.shape[1] // LANE):
        found = pick(table[:, part * LANE : (part + 1) * LANE], low)
        result = jnp.where(index >= part * LANE, found, result)
    return result


def split3(x):
    high = x.astype(jnp.bfloat16)
    rest = x - high.astype(jnp.float32)
    middle = rest.astype(jnp.bfloat16)
    low = (rest - middle.astype(jnp.float32)).astype(jnp.bfloat16)
    return high, middle, low


def owner_table(owner, row, owners):
    q_dev, cands = owner.shape
    width = -(-owners // LANE) * LANE
    lane = lax.broadcasted_iota(jnp.int32, (q_dev, width), 1)
    table = jnp.full((q_dev, width), -1, jnp.int32)
    for c in range(cands):
        table = jnp.where(lane == owner[:, c : c + 1], row[:, c : c + 1], table)
    return table


def before(table):
    asked = (table >= 0).astype(jnp.int32)
    rows = [jnp.zeros_like(asked[0:1])]
    for q in range(1, table.shape[0]):
        rows.append(rows[-1] + asked[q - 1 : q])
    return jnp.concatenate(rows, axis=0)


def layout_of(pair_count, owners, width):
    capacity = max(2, pair_count // owners)
    parts = max(
        p for p in range(1, 9) if p == 1 or (p * capacity <= SUB and width % (p * LANE) == 0)
    )
    return capacity, parts


def ids_kernel(capacity, parts, owner_ref, row_ref, out_ref):
    owners = out_ref.shape[0]
    table = owner_table(owner_ref[...], row_ref[...], owners)
    rank = before(table)
    rows = []
    for s in range(capacity):
        rows.append(jnp.max(jnp.where(rank == s, table, -1), axis=0, keepdims=True))
    rows = rows * parts
    rows += [jnp.full_like(rows[0], -1)] * (SUB - len(rows))
    packed = jnp.concatenate(rows, axis=0)
    for block in range(packed.shape[1] // LANE):
        square = jnp.concatenate(
            [packed[:, block * LANE : (block + 1) * LANE]]
            + [jnp.zeros((LANE - SUB, LANE), jnp.int32)],
            axis=0,
        )
        count = min(LANE, owners - block * LANE)
        turned = square.T[:count]
        out_ref[block * LANE : block * LANE + count] = turned.reshape(count, 1, LANE)


def rows_kernel(capacity, parts, ids_ref, vectors_ref, out_ref):
    sources, slots = out_ref.shape[0], out_ref.shape[1]
    count, width = vectors_ref.shape
    piece = width // parts
    shape = (sources, slots, LANE)
    lane = lax.broadcasted_iota(jnp.int32, shape, 2)
    own = jnp.where(lane == lax.broadcasted_iota(jnp.int32, shape, 1), ids_ref[...], 0)
    ids = jnp.sum(own, axis=2, keepdims=True).reshape(sources * slots, 1)
    pieces = []
    for block in range(count // LANE):
        lane = lax.broadcasted_iota(jnp.int32, (sources * slots, LANE), 1) + block * LANE
        pieces.append(jnp.where(ids == lane, 1.0, 0.0).astype(jnp.bfloat16))
    chosen = jnp.concatenate(pieces, axis=1)
    slot = lax.broadcasted_iota(jnp.int32, (sources * slots, piece), 0) % slots
    result = None
    for part in range(parts):
        vectors = vectors_ref[:, part * piece : (part + 1) * piece].astype(jnp.bfloat16)
        found = jnp.dot(chosen, vectors, preferred_element_type=jnp.float32)
        result = found if part == 0 else jnp.where(slot >= part * capacity, found, result)
    out_ref[...] = result.reshape(sources, slots, piece).astype(jnp.bfloat16)


def final_kernel(capacity, parts, owner_ref, row_ref, queries_ref, rows_ref, out_ref):
    owners, slots, piece = rows_ref.shape
    q_dev, cands = out_ref.shape
    rows = rows_ref[...].reshape(owners * slots, piece)
    total = None
    for part in range(parts):
        x = queries_ref[:, part * piece : (part + 1) * piece]
        stacked = jnp.concatenate(split3(x), axis=0)
        product = lax.dot_general(
            stacked, rows, (((1,), (1,)), ((), ())), preferred_element_type=jnp.float32
        )
        scores = product[:q_dev] + product[q_dev : 2 * q_dev] + product[2 * q_dev :]
        if part:
            width = scores.shape[1]
            scores = pltpu.roll(scores, width - part * capacity, axis=1)
        total = scores if part == 0 else total + scores
    owner = owner_ref[...]
    padded = jnp.concatenate([owner, jnp.zeros((q_dev, LANE - cands), jnp.int32)], axis=1)
    rank = before(owner_table(owner, row_ref[...], owners))
    place = padded * slots + pick_wide(rank, padded)
    out_ref[...] = pick_wide(total, place)[:, :cands]


def join_kernel(*refs):
    rows = refs[0].shape[0]
    for n, ref in enumerate(refs[:-1]):
        refs[-1][n * rows : (n + 1) * rows] = ref[...]


def lists_kernel(lists, probes_ref, out_ref):
    total = probes_ref.shape[1]
    width = out_ref.shape[1]
    shard = lax.axis_index("shard")
    wanted = shard * lists + lax.broadcasted_iota(jnp.int32, (lists, total), 0)
    hit = jnp.zeros((lists, total), jnp.int32)
    for p in range(probes_ref.shape[0]):
        hit = jnp.where(probes_ref[p : p + 1, :] == wanted, 1, hit)
    upto = lax.broadcasted_iota(jnp.int32, (total, total), 0) >= lax.broadcasted_iota(
        jnp.int32, (total, total), 1
    )
    running = lax.dot_general(
        upto.astype(jnp.float32).astype(jnp.bfloat16),
        hit.astype(jnp.float32).astype(jnp.bfloat16),
        (((1,), (1,)), ((), ())),
        preferred_element_type=jnp.float32,
    )
    rank = lax.broadcasted_iota(jnp.int32, (total, width), 1).astype(jnp.float32)
    position = lax.broadcasted_iota(jnp.int32, (lists, total), 1)
    last = jnp.max(jnp.where(hit > 0, position, 0), axis=1, keepdims=True)
    counts = jnp.sum(hit, axis=1, keepdims=True)
    found = []
    for n in range(lists):
        passed = jnp.where(running[:, n : n + 1] <= rank, 1.0, 0.0)
        found.append(jnp.sum(passed, axis=0, keepdims=True))
    found = jnp.concatenate(found, axis=0).astype(jnp.int32)
    place = lax.broadcasted_iota(jnp.int32, (lists, width), 1)
    found = jnp.where(place < counts, found, last)
    found = jnp.where(place == width - 1, counts, found)
    out_ref[...] = found


def pq_kernel(q_dev, pieces, unroll, lists_hbm, codebook_ref, wide_codes, *refs):
    number = len(pieces)
    chunk_refs, (out_ref, queries, table, codes, lists_s, sems) = (
        refs[:number],
        refs[number:],
    )
    lists, subs, entries = codes.shape
    total = queries.shape[0]
    centres = codebook_ref.shape[1]
    rows = 2 * SUB
    blocks = subs // rows
    shard = lax.axis_index("shard")

    send = pltpu.make_async_copy(lists_hbm, lists_s, sems.at[1])
    send.start()

    for (offset, begin, size), ref in zip(pieces, chunk_refs):
        start = 0 if offset is None else jnp.bitwise_xor(shard, offset) * q_dev
        queries[pl.ds(pl.multiple_of(start, q_dev), size), :] = ref[begin : begin + size, :]

    out_ref[...] = jnp.zeros(out_ref.shape, jnp.float32)

    half = LANE // 2
    lane = lax.broadcasted_iota(jnp.int32, (total, LANE), 1)
    inside = lax.broadcasted_iota(jnp.int32, (1, SUB, LANE), 2) % half // (half // SUB)
    own = jnp.where(inside == lax.broadcasted_iota(jnp.int32, (1, SUB, LANE), 1), 1.0, 0.0)

    def columns(k, carry):
        x = queries[:, pl.ds(pl.multiple_of(k * LANE, LANE), LANE)]
        swapped = pltpu.roll(x, half, axis=1)
        products = []
        for side in range(2):
            wide = jnp.where((lane < half) == (side == 0), x, swapped)
            high = wide.astype(jnp.bfloat16).astype(jnp.float32)
            terms = []
            for term in (high, wide - high):
                spread = (term[:, None, :] * own).reshape(total * SUB, LANE)
                terms.append(spread.astype(jnp.bfloat16))
            c = codebook_ref[pl.ds(pl.multiple_of(k * LANE + side * half, half), half), :]
            c_high = c.astype(jnp.bfloat16)
            c_low = (c - c_high.astype(jnp.float32)).astype(jnp.bfloat16)
            weights = jnp.concatenate([c_high, c_low, c_high, c_low], axis=0)
            product = jnp.dot(
                jnp.concatenate(terms, axis=1), weights, preferred_element_type=jnp.float32
            )
            products.append(product.reshape(total, SUB, centres))
        table[:, k] = jnp.concatenate(products, axis=1).astype(jnp.bfloat16)
        return carry

    lax.fori_loop(0, blocks, columns, 0)
    for n in range(lists):
        codes[n] = wide_codes[n].astype(jnp.int16)
    send.wait()
    halves = entries // LANE
    width = lists_s.shape[1]

    def emit(n, chosen, sums):
        for u in range(unroll):
            line = [
                jnp.sum(s, axis=0, keepdims=True) for s in sums[u * halves : (u + 1) * halves]
            ]
            out_ref[n, pl.ds(chosen[u], 1), :] = jnp.concatenate(line, axis=1)

    def one_list(n, carry):
        count = lists_s[n, width - 1]

        def some(step, inner):
            chosen = tuple(lists_s[n, step * unroll + u] for u in range(unroll))
            sums = [None] * (unroll * halves)
            for i in range(blocks):
                for h in range(halves):
                    code = codes[n, i * rows : (i + 1) * rows, h * LANE : (h + 1) * LANE]
                    low = jnp.bitwise_and(code, jnp.int16(LANE - 1))
                    for u in range(unroll):
                        value = pick(table[chosen[u], i, :, 0:LANE], low)
                        for part in range(1, centres // LANE):
                            other = pick(
                                table[chosen[u], i, :, part * LANE : (part + 1) * LANE], low
                            )
                            value = jnp.where(code >= jnp.int16(part * LANE), other, value)
                        value = value.astype(jnp.float32)
                        value = value[:SUB] + value[SUB:]
                        at = u * halves + h
                        sums[at] = value if i == 0 else sums[at] + value
                if i == 1:
                    emit(*inner)
            return n, chosen, tuple(sums)

        return lax.fori_loop(0, (count + unroll - 1) // unroll, some, carry)

    first = (
        jnp.int32(0),
        (jnp.int32(0),) * unroll,
        (jnp.zeros((SUB, LANE), jnp.float32),) * (unroll * halves),
    )
    emit(*lax.fori_loop(0, lists, one_list, first))


def whole(memory=pltpu.VMEM):
    return pl.BlockSpec(memory_space=memory)


def per_device(queries, codebook, pq_codes, probes, vectors, cand_owner, cand_row):
    shards = lax.axis_size("shard")
    owners = lax.axis_size("group") * shards
    q_dev, width = queries.shape
    cands = cand_owner.shape[1]
    subs, centres, dims = codebook.shape
    lists, _, entries = pq_codes.shape
    total = q_dev * shards
    capacity, parts = layout_of(q_dev * cands, owners, width)
    unroll = 8

    ids = pl.pallas_call(
        lambda *refs: ids_kernel(capacity, parts, *refs),
        out_shape=jax.ShapeDtypeStruct((owners, 1, LANE), jnp.int32),
        in_specs=[whole()] * 2,
        out_specs=whole(),
        name="ids",
        cost_estimate=pl.CostEstimate(flops=10**9, bytes_accessed=6 << 20, transcendentals=0),
    )(cand_owner, cand_row)
    list_width = -(-(total + unroll + 1) // LANE) * LANE
    grouping = pl.pallas_call(
        lambda *refs: lists_kernel(lists, *refs),
        out_shape=jax.ShapeDtypeStruct((lists, list_width), jnp.int32),
        in_specs=[whole()],
        out_specs=whole(),
        name="groups",
        compiler_params=pltpu.CompilerParams(vmem_limit_bytes=4 << 20),
        cost_estimate=pl.CostEstimate(flops=10**9, bytes_accessed=12 << 20, transcendentals=0),
    )
    groups = grouping(probes.T)
    own, groups = lax.optimization_barrier((queries, groups))
    asked = lax.all_to_all(ids, AXES, split_axis=0, concat_axis=0, tiled=True)

    near = [queries]
    if shards == 8:
        near += [
            lax.ppermute(own, "shard", [(i, i ^ k) for i in range(shards)])
            for k in range(2, shards, 2)
        ]
    else:
        gathered = lax.all_gather(queries, "shard", axis=0, tiled=True)

    rows = pl.pallas_call(
        lambda *refs: rows_kernel(capacity, parts, *refs),
        out_shape=jax.ShapeDtypeStruct((owners, SUB, width // parts), jnp.bfloat16),
        in_specs=[whole()] * 2,
        out_specs=whole(),
        name="rows",
        compiler_params=pltpu.CompilerParams(vmem_limit_bytes=16 << 20),
        cost_estimate=pl.CostEstimate(flops=10**9, bytes_accessed=4 << 20, transcendentals=0),
    )(asked, vectors)
    returned = lax.all_to_all(rows, AXES, split_axis=0, concat_axis=0, tiled=True)
    pieces, chunks = [], []
    if shards == 8:
        joined = pl.pallas_call(
            join_kernel,
            out_shape=jax.ShapeDtypeStruct((len(near) * q_dev, width), jnp.float32),
            in_specs=[whole()] * len(near),
            out_specs=whole(),
            name="join",
            compiler_params=pltpu.CompilerParams(vmem_limit_bytes=4 << 20),
            cost_estimate=pl.CostEstimate(flops=10**9, bytes_accessed=16 << 20, transcendentals=0),
        )(*near)
        other = lax.ppermute(joined, "shard", [(i, i ^ 1) for i in range(shards)])
        for side, chunk in enumerate((joined, other)):
            for n in range(len(near)):
                chunks.append(chunk)
                pieces.append((2 * n ^ side, n * q_dev, q_dev))
    else:
        pieces.append((None, 0, total))
        chunks.append(gathered)

    pq = pl.pallas_call(
        lambda *refs: pq_kernel(q_dev, pieces, unroll, *refs),
        out_shape=jax.ShapeDtypeStruct((lists, total, entries), jnp.float32),
        in_specs=[whole(pl.ANY)] + [whole()] * 2 + [whole()] * len(chunks),
        out_specs=whole(),
        scratch_shapes=[
            pltpu.VMEM((total, width), jnp.float32),
            pltpu.VMEM((total, subs // SUB // 2, 2 * SUB, centres), jnp.bfloat16),
            pltpu.VMEM((lists, subs, entries), jnp.int16),
            pltpu.SMEM((lists, list_width), jnp.int32),
            pltpu.SemaphoreType.DMA((3,)),
        ],
        name="pq",
        compiler_params=pltpu.CompilerParams(
            vmem_limit_bytes=14300000
        ),
        cost_estimate=pl.CostEstimate(
            flops=10**10, bytes_accessed=30 << 20, transcendentals=0
        ),
    )(
        groups,
        codebook.transpose(0, 2, 1).reshape(subs * dims, centres),
        pq_codes,
        *chunks,
    )

    rerank = pl.pallas_call(
        lambda *refs: final_kernel(capacity, parts, *refs),
        out_shape=jax.ShapeDtypeStruct((q_dev, cands), jnp.float32),
        in_specs=[whole()] * 4,
        out_specs=whole(),
        name="final",
        compiler_params=pltpu.CompilerParams(vmem_limit_bytes=8 << 20),
    )(cand_owner, cand_row, queries, returned)
    return pq.transpose(0, 2, 1), rerank


def solution(mesh):
    in_specs = (
        P(AXES, None),
        P(),
        P(AXES, None, None),
        P("group", None),
        P(AXES, None),
        P(AXES, None),
        P(AXES, None),
    )
    out_specs = (P(AXES, None, None), P(AXES, None))
    return jax.shard_map(
        per_device, mesh=mesh, in_specs=in_specs, out_specs=out_specs, check_vma=False
    )
```

```python
import jax
import jax.numpy as jnp
from jax import lax
from jax.experimental import pallas as pl
from jax.experimental.pallas import tpu as pltpu
from jax.sharding import PartitionSpec as P


AXES = ("group", "shard")
SUB = 8
LANE = 128
GATHER = lax.GatherDimensionNumbers(
    offset_dims=(),
    collapsed_slice_dims=(1,),
    start_index_map=(1,),
    operand_batching_dims=(0,),
    start_indices_batching_dims=(0,),
)


def pick(table, index):
    return lax.gather(
        table, index[..., None], GATHER, (1, 1), mode=lax.GatherScatterMode.PROMISE_IN_BOUNDS
    )


def pick_wide(table, index):
    low = jnp.bitwise_and(index, LANE - 1)
    result = pick(table[:, :LANE], low)
    for part in range(1, table.shape[1] // LANE):
        found = pick(table[:, part * LANE : (part + 1) * LANE], low)
        result = jnp.where(index >= part * LANE, found, result)
    return result


def split3(x):
    high = x.astype(jnp.bfloat16)
    rest = x - high.astype(jnp.float32)
    middle = rest.astype(jnp.bfloat16)
    low = (rest - middle.astype(jnp.float32)).astype(jnp.bfloat16)
    return high, middle, low


def owner_table(owner, row, owners):
    q_dev, cands = owner.shape
    width = -(-owners // LANE) * LANE
    lane = lax.broadcasted_iota(jnp.int32, (q_dev, width), 1)
    table = jnp.full((q_dev, width), -1, jnp.int32)
    for c in range(cands):
        table = jnp.where(lane == owner[:, c : c + 1], row[:, c : c + 1], table)
    return table


def before(table):
    asked = (table >= 0).astype(jnp.int32)
    rows = [jnp.zeros_like(asked[0:1])]
    for q in range(1, table.shape[0]):
        rows.append(rows[-1] + asked[q - 1 : q])
    return jnp.concatenate(rows, axis=0)


def layout_of(pair_count, owners, width):
    capacity = max(2, pair_count // owners)
    parts = max(
        p for p in range(1, 9) if p == 1 or (p * capacity <= SUB and width % (p * LANE) == 0)
    )
    return capacity, parts


def ids_kernel(capacity, parts, owner_ref, row_ref, out_ref):
    owners = out_ref.shape[0]
    table = owner_table(owner_ref[...], row_ref[...], owners)
    rank = before(table)
    rows = []
    for s in range(capacity):
        rows.append(jnp.max(jnp.where(rank == s, table, -1), axis=0, keepdims=True))
    rows = rows * parts
    rows += [jnp.full_like(rows[0], -1)] * (SUB - len(rows))
    packed = jnp.concatenate(rows, axis=0)
    for block in range(packed.shape[1] // LANE):
        square = jnp.concatenate(
            [packed[:, block * LANE : (block + 1) * LANE]]
            + [jnp.zeros((LANE - SUB, LANE), jnp.int32)],
            axis=0,
        )
        count = min(LANE, owners - block * LANE)
        turned = square.T[:count]
        out_ref[block * LANE : block * LANE + count] = turned.reshape(count, 1, LANE)


def paired_rows_kernel(ids_ref, vectors_ref, out_ref):
    sources, slots, piece = out_ref.shape
    count = vectors_ref.shape[0]
    pairs = sources // 2
    shape = (pairs, SUB, LANE)
    lane = lax.broadcasted_iota(jnp.int32, shape, 2)
    row = lax.broadcasted_iota(jnp.int32, shape, 1)
    ids = ids_ref[...].reshape(pairs, 2, 1, LANE)
    mine = jnp.where(row < SUB // 2, ids[:, 0], ids[:, 1])
    mine = jnp.where(lane == row % (SUB // 2), mine, 0)
    wanted = jnp.sum(mine, axis=2, keepdims=True).reshape(pairs * SUB, 1)
    chosen = []
    for block in range(count // LANE):
        lane = lax.broadcasted_iota(jnp.int32, (pairs * SUB, LANE), 1) + block * LANE
        chosen.append(jnp.where(wanted == lane, 1.0, 0.0).astype(jnp.bfloat16))
    chosen = jnp.concatenate(chosen, axis=1)
    found = []
    for part in range(2):
        vectors = vectors_ref[:, part * piece : (part + 1) * piece].astype(jnp.bfloat16)
        product = jnp.dot(chosen, vectors, preferred_element_type=jnp.float32)
        found.append(product.reshape(pairs, SUB, piece))
    swapped = [pltpu.roll(x, SUB // 2, axis=1) for x in found]
    upper = lax.broadcasted_iota(jnp.int32, (pairs, SUB, piece), 1) < SUB // 2
    even = jnp.where(upper, found[0], swapped[1])
    odd = jnp.where(upper, swapped[0], found[1])
    result = jnp.stack([even, odd], axis=1).reshape(sources, slots, piece)
    out_ref[...] = result.astype(jnp.bfloat16)


def rows_kernel(capacity, parts, ids_ref, vectors_ref, out_ref):
    if capacity * 2 == SUB and parts == 2 and out_ref.shape[0] % 2 == 0:
        return paired_rows_kernel(ids_ref, vectors_ref, out_ref)
    sources, slots = out_ref.shape[0], out_ref.shape[1]
    count, width = vectors_ref.shape
    piece = width // parts
    shape = (sources, slots, LANE)
    lane = lax.broadcasted_iota(jnp.int32, shape, 2)
    own = jnp.where(lane == lax.broadcasted_iota(jnp.int32, shape, 1), ids_ref[...], 0)
    ids = jnp.sum(own, axis=2, keepdims=True).reshape(sources * slots, 1)
    pieces = []
    for block in range(count // LANE):
        lane = lax.broadcasted_iota(jnp.int32, (sources * slots, LANE), 1) + block * LANE
        pieces.append(jnp.where(ids == lane, 1.0, 0.0).astype(jnp.bfloat16))
    chosen = jnp.concatenate(pieces, axis=1)
    slot = lax.broadcasted_iota(jnp.int32, (sources * slots, piece), 0) % slots
    result = None
    for part in range(parts):
        vectors = vectors_ref[:, part * piece : (part + 1) * piece].astype(jnp.bfloat16)
        found = jnp.dot(chosen, vectors, preferred_element_type=jnp.float32)
        result = found if part == 0 else jnp.where(slot >= part * capacity, found, result)
    out_ref[...] = result.reshape(sources, slots, piece).astype(jnp.bfloat16)


def final_kernel(capacity, parts, owner_ref, row_ref, queries_ref, rows_ref, out_ref):
    owners, slots, piece = rows_ref.shape
    q_dev, cands = out_ref.shape
    rows = rows_ref[...].reshape(owners * slots, piece)
    total = None
    for part in range(parts):
        x = queries_ref[:, part * piece : (part + 1) * piece]
        stacked = jnp.concatenate(split3(x), axis=0)
        product = lax.dot_general(
            stacked, rows, (((1,), (1,)), ((), ())), preferred_element_type=jnp.float32
        )
        scores = product[:q_dev] + product[q_dev : 2 * q_dev] + product[2 * q_dev :]
        if part:
            width = scores.shape[1]
            scores = pltpu.roll(scores, width - part * capacity, axis=1)
        total = scores if part == 0 else total + scores
    owner = owner_ref[...]
    padded = jnp.concatenate([owner, jnp.zeros((q_dev, LANE - cands), jnp.int32)], axis=1)
    rank = before(owner_table(owner, row_ref[...], owners))
    place = padded * slots + pick_wide(rank, padded)
    out_ref[...] = pick_wide(total, place)[:, :cands]


def join_kernel(*refs):
    rows = refs[0].shape[0]
    for n, ref in enumerate(refs[:-1]):
        refs[-1][n * rows : (n + 1) * rows] = ref[...]


def lists_kernel(lists, probes_ref, out_ref):
    total = probes_ref.shape[1]
    width = out_ref.shape[1]
    shard = lax.axis_index("shard")
    wanted = shard * lists + lax.broadcasted_iota(jnp.int32, (lists, total), 0)
    hit = jnp.zeros((lists, total), jnp.int32)
    for p in range(probes_ref.shape[0]):
        hit = jnp.where(probes_ref[p : p + 1, :] == wanted, 1, hit)
    upto = lax.broadcasted_iota(jnp.int32, (total, total), 0) >= lax.broadcasted_iota(
        jnp.int32, (total, total), 1
    )
    running = lax.dot_general(
        upto.astype(jnp.float32).astype(jnp.bfloat16),
        hit.astype(jnp.float32).astype(jnp.bfloat16),
        (((1,), (1,)), ((), ())),
        preferred_element_type=jnp.float32,
    )
    rank = lax.broadcasted_iota(jnp.int32, (total, width), 1).astype(jnp.float32)
    position = lax.broadcasted_iota(jnp.int32, (lists, total), 1)
    last = jnp.max(jnp.where(hit > 0, position, 0), axis=1, keepdims=True)
    counts = jnp.sum(hit, axis=1, keepdims=True)
    found = []
    for n in range(lists):
        passed = jnp.where(running[:, n : n + 1] <= rank, 1.0, 0.0)
        found.append(jnp.sum(passed, axis=0, keepdims=True))
    found = jnp.concatenate(found, axis=0).astype(jnp.int32)
    place = lax.broadcasted_iota(jnp.int32, (lists, width), 1)
    found = jnp.where(place < counts, found, last)
    found = jnp.where(place == width - 1, counts, found)
    out_ref[...] = found


def pq_kernel(q_dev, pieces, unroll, lists_hbm, codebook_ref, wide_codes, *refs):
    number = len(pieces)
    chunk_refs, (out_ref, queries, table, codes, lists_s, sems) = (
        refs[:number],
        refs[number:],
    )
    lists, subs, entries = codes.shape
    total = queries.shape[0]
    centres = codebook_ref.shape[1]
    rows = 2 * SUB
    blocks = subs // rows
    shard = lax.axis_index("shard")

    send = pltpu.make_async_copy(lists_hbm, lists_s, sems.at[1])
    send.start()

    for (offset, begin, size), ref in zip(pieces, chunk_refs):
        start = 0 if offset is None else jnp.bitwise_xor(shard, offset) * q_dev
        queries[pl.ds(pl.multiple_of(start, q_dev), size), :] = ref[begin : begin + size, :]

    out_ref[...] = jnp.zeros(out_ref.shape, jnp.float32)

    half = LANE // 2
    lane = lax.broadcasted_iota(jnp.int32, (total, LANE), 1)
    inside = lax.broadcasted_iota(jnp.int32, (1, SUB, LANE), 2) % half // (half // SUB)
    own = jnp.where(inside == lax.broadcasted_iota(jnp.int32, (1, SUB, LANE), 1), 1.0, 0.0)

    def columns(k, carry):
        x = queries[:, pl.ds(pl.multiple_of(k * LANE, LANE), LANE)]
        swapped = pltpu.roll(x, half, axis=1)
        products = []
        for side in range(2):
            wide = jnp.where((lane < half) == (side == 0), x, swapped)
            high = wide.astype(jnp.bfloat16).astype(jnp.float32)
            terms = []
            for term in (high, wide - high):
                spread = (term[:, None, :] * own).reshape(total * SUB, LANE)
                terms.append(spread.astype(jnp.bfloat16))
            c = codebook_ref[pl.ds(pl.multiple_of(k * LANE + side * half, half), half), :]
            c_high = c.astype(jnp.bfloat16)
            c_low = (c - c_high.astype(jnp.float32)).astype(jnp.bfloat16)
            weights = jnp.concatenate([c_high, c_low, c_high, c_low], axis=0)
            product = jnp.dot(
                jnp.concatenate(terms, axis=1), weights, preferred_element_type=jnp.float32
            )
            products.append(product.reshape(total, SUB, centres))
        table[:, k] = jnp.concatenate(products, axis=1).astype(jnp.bfloat16)
        return carry

    lax.fori_loop(0, blocks, columns, 0)
    for n in range(lists):
        codes[n] = wide_codes[n].astype(jnp.int16)
    send.wait()
    halves = entries // LANE
    width = lists_s.shape[1]

    def emit(n, chosen, sums):
        for u in range(unroll):
            line = [
                jnp.sum(s, axis=0, keepdims=True) for s in sums[u * halves : (u + 1) * halves]
            ]
            out_ref[n, pl.ds(chosen[u], 1), :] = jnp.concatenate(line, axis=1)

    def one_list(n, carry):
        count = lists_s[n, width - 1]

        def some(step, inner):
            chosen = tuple(lists_s[n, step * unroll + u] for u in range(unroll))
            sums = [None] * (unroll * halves)
            for i in range(blocks):
                for h in range(halves):
                    code = codes[n, i * rows : (i + 1) * rows, h * LANE : (h + 1) * LANE]
                    low = jnp.bitwise_and(code, jnp.int16(LANE - 1))
                    for u in range(unroll):
                        value = pick(table[chosen[u], i, :, 0:LANE], low)
                        for part in range(1, centres // LANE):
                            other = pick(
                                table[chosen[u], i, :, part * LANE : (part + 1) * LANE], low
                            )
                            value = jnp.where(code >= jnp.int16(part * LANE), other, value)
                        value = value.astype(jnp.float32)
                        value = value[:SUB] + value[SUB:]
                        at = u * halves + h
                        sums[at] = value if i == 0 else sums[at] + value
                if i == 1:
                    emit(*inner)
            return n, chosen, tuple(sums)

        return lax.fori_loop(0, (count + unroll - 1) // unroll, some, carry)

    first = (
        jnp.int32(0),
        (jnp.int32(0),) * unroll,
        (jnp.zeros((SUB, LANE), jnp.float32),) * (unroll * halves),
    )
    emit(*lax.fori_loop(0, lists, one_list, first))


def whole(memory=pltpu.VMEM):
    return pl.BlockSpec(memory_space=memory)


def per_device(queries, codebook, pq_codes, probes, vectors, cand_owner, cand_row):
    shards = lax.axis_size("shard")
    owners = lax.axis_size("group") * shards
    q_dev, width = queries.shape
    cands = cand_owner.shape[1]
    subs, centres, dims = codebook.shape
    lists, _, entries = pq_codes.shape
    total = q_dev * shards
    capacity, parts = layout_of(q_dev * cands, owners, width)
    unroll = 8

    ids = pl.pallas_call(
        lambda *refs: ids_kernel(capacity, parts, *refs),
        out_shape=jax.ShapeDtypeStruct((owners, 1, LANE), jnp.int32),
        in_specs=[whole()] * 2,
        out_specs=whole(),
        name="ids",
        cost_estimate=pl.CostEstimate(flops=10**9, bytes_accessed=6 << 20, transcendentals=0),
    )(cand_owner, cand_row)
    list_width = -(-(total + unroll + 1) // LANE) * LANE
    grouping = pl.pallas_call(
        lambda *refs: lists_kernel(lists, *refs),
        out_shape=jax.ShapeDtypeStruct((lists, list_width), jnp.int32),
        in_specs=[whole()],
        out_specs=whole(),
        name="groups",
        compiler_params=pltpu.CompilerParams(vmem_limit_bytes=4 << 20),
        cost_estimate=pl.CostEstimate(flops=10**9, bytes_accessed=12 << 20, transcendentals=0),
    )
    groups = grouping(probes.T)
    own, groups = lax.optimization_barrier((queries, groups))
    asked = lax.all_to_all(ids, AXES, split_axis=0, concat_axis=0, tiled=True)

    near = [queries]
    if shards == 8:
        near += [
            lax.ppermute(own, "shard", [(i, i ^ k) for i in range(shards)])
            for k in range(2, shards, 2)
        ]
    else:
        gathered = lax.all_gather(queries, "shard", axis=0, tiled=True)

    rows = pl.pallas_call(
        lambda *refs: rows_kernel(capacity, parts, *refs),
        out_shape=jax.ShapeDtypeStruct((owners, SUB, width // parts), jnp.bfloat16),
        in_specs=[whole()] * 2,
        out_specs=whole(),
        name="rows",
        compiler_params=pltpu.CompilerParams(vmem_limit_bytes=16 << 20),
        cost_estimate=pl.CostEstimate(flops=10**9, bytes_accessed=4 << 20, transcendentals=0),
    )(asked, vectors)
    returned = lax.all_to_all(rows, AXES, split_axis=0, concat_axis=0, tiled=True)
    pieces, chunks = [], []
    if shards == 8:
        joined = pl.pallas_call(
            join_kernel,
            out_shape=jax.ShapeDtypeStruct((len(near) * q_dev, width), jnp.float32),
            in_specs=[whole()] * len(near),
            out_specs=whole(),
            name="join",
            compiler_params=pltpu.CompilerParams(vmem_limit_bytes=4 << 20),
            cost_estimate=pl.CostEstimate(flops=10**9, bytes_accessed=16 << 20, transcendentals=0),
        )(*near)
        other = lax.ppermute(joined, "shard", [(i, i ^ 1) for i in range(shards)])
        for side, chunk in enumerate((joined, other)):
            for n in range(len(near)):
                chunks.append(chunk)
                pieces.append((2 * n ^ side, n * q_dev, q_dev))
    else:
        pieces.append((None, 0, total))
        chunks.append(gathered)

    pq = pl.pallas_call(
        lambda *refs: pq_kernel(q_dev, pieces, unroll, *refs),
        out_shape=jax.ShapeDtypeStruct((lists, total, entries), jnp.float32),
        in_specs=[whole(pl.ANY)] + [whole()] * 2 + [whole()] * len(chunks),
        out_specs=whole(),
        scratch_shapes=[
            pltpu.VMEM((total, width), jnp.float32),
            pltpu.VMEM((total, subs // SUB // 2, 2 * SUB, centres), jnp.bfloat16),
            pltpu.VMEM((lists, subs, entries), jnp.int16),
            pltpu.SMEM((lists, list_width), jnp.int32),
            pltpu.SemaphoreType.DMA((3,)),
        ],
        name="pq",
        compiler_params=pltpu.CompilerParams(
            vmem_limit_bytes=14300000
        ),
        cost_estimate=pl.CostEstimate(
            flops=10**10, bytes_accessed=30 << 20, transcendentals=0
        ),
    )(
        groups,
        codebook.transpose(0, 2, 1).reshape(subs * dims, centres),
        pq_codes,
        *chunks,
    )

    rerank = pl.pallas_call(
        lambda *refs: final_kernel(capacity, parts, *refs),
        out_shape=jax.ShapeDtypeStruct((q_dev, cands), jnp.float32),
        in_specs=[whole()] * 4,
        out_specs=whole(),
        name="final",
        compiler_params=pltpu.CompilerParams(vmem_limit_bytes=8 << 20),
    )(cand_owner, cand_row, queries, returned)
    return pq.transpose(0, 2, 1), rerank


def solution(mesh):
    in_specs = (
        P(AXES, None),
        P(),
        P(AXES, None, None),
        P("group", None),
        P(AXES, None),
        P(AXES, None),
        P(AXES, None),
    )
    out_specs = (P(AXES, None, None), P(AXES, None))
    return jax.shard_map(
        per_device, mesh=mesh, in_specs=in_specs, out_specs=out_specs, check_vma=False
    )
```

```python
import jax
import jax.numpy as jnp
from jax import lax
from jax.experimental import pallas as pl
from jax.experimental.pallas import tpu as pltpu
from jax.sharding import PartitionSpec as P


AXES = ("group", "shard")
SUB = 8
LANE = 128
GATHER = lax.GatherDimensionNumbers(
    offset_dims=(),
    collapsed_slice_dims=(1,),
    start_index_map=(1,),
    operand_batching_dims=(0,),
    start_indices_batching_dims=(0,),
)


def pick(table, index):
    return lax.gather(
        table, index[..., None], GATHER, (1, 1), mode=lax.GatherScatterMode.PROMISE_IN_BOUNDS
    )


def pick_wide(table, index):
    low = jnp.bitwise_and(index, LANE - 1)
    result = pick(table[:, :LANE], low)
    for part in range(1, table.shape[1] // LANE):
        found = pick(table[:, part * LANE : (part + 1) * LANE], low)
        result = jnp.where(index >= part * LANE, found, result)
    return result


def split3(x):
    high = x.astype(jnp.bfloat16)
    rest = x - high.astype(jnp.float32)
    middle = rest.astype(jnp.bfloat16)
    low = (rest - middle.astype(jnp.float32)).astype(jnp.bfloat16)
    return high, middle, low


def owner_table(owner, row, owners):
    q_dev, cands = owner.shape
    width = -(-owners // LANE) * LANE
    lane = lax.broadcasted_iota(jnp.int32, (q_dev, width), 1)
    table = jnp.full((q_dev, width), -1, jnp.int32)
    for c in range(cands):
        table = jnp.where(lane == owner[:, c : c + 1], row[:, c : c + 1], table)
    return table


def before(table):
    asked = (table >= 0).astype(jnp.int32)
    rows = [jnp.zeros_like(asked[0:1])]
    for q in range(1, table.shape[0]):
        rows.append(rows[-1] + asked[q - 1 : q])
    return jnp.concatenate(rows, axis=0)


def layout_of(pair_count, owners, width):
    capacity = max(2, pair_count // owners)
    parts = max(
        p for p in range(1, 9) if p == 1 or (p * capacity <= SUB and width % (p * LANE) == 0)
    )
    return capacity, parts


def ids_kernel(capacity, parts, owner_ref, row_ref, out_ref):
    owners = out_ref.shape[0]
    table = owner_table(owner_ref[...], row_ref[...], owners)
    rank = before(table)
    rows = []
    for s in range(capacity):
        rows.append(jnp.max(jnp.where(rank == s, table, -1), axis=0, keepdims=True))
    rows = rows * parts
    rows += [jnp.full_like(rows[0], -1)] * (SUB - len(rows))
    packed = jnp.concatenate(rows, axis=0)
    for block in range(packed.shape[1] // LANE):
        square = jnp.concatenate(
            [packed[:, block * LANE : (block + 1) * LANE]]
            + [jnp.zeros((LANE - SUB, LANE), jnp.int32)],
            axis=0,
        )
        count = min(LANE, owners - block * LANE)
        turned = square.T[:count]
        out_ref[block * LANE : block * LANE + count] = turned.reshape(count, 1, LANE)


def paired_rows_kernel(ids_ref, vectors_ref, out_ref, buffer, sems):
    sources, slots, piece = out_ref.shape
    count = vectors_ref.shape[0]
    pairs = sources // 2
    shape = (pairs, SUB, LANE)
    lane = lax.broadcasted_iota(jnp.int32, shape, 2)
    row = lax.broadcasted_iota(jnp.int32, shape, 1)
    ids = ids_ref[...].reshape(pairs, 2, 1, LANE)
    mine = jnp.where(row < SUB // 2, ids[:, 0], ids[:, 1])
    mine = jnp.where(lane == row % (SUB // 2), mine, 0)
    wanted = jnp.sum(mine, axis=2, keepdims=True).reshape(pairs * SUB, 1)
    chosen = []
    for block in range(count // LANE):
        lane = lax.broadcasted_iota(jnp.int32, (pairs * SUB, LANE), 1) + block * LANE
        chosen.append(jnp.where(wanted == lane, 1.0, 0.0).astype(jnp.bfloat16))
    chosen = jnp.concatenate(chosen, axis=1)
    upper = lax.broadcasted_iota(jnp.int32, (pairs, SUB, LANE), 1) < SUB // 2
    copies = []
    for step in range(piece // LANE):
        found = []
        for part in range(2):
            start = part * piece + step * LANE
            found.append(vectors_ref[:, start : start + LANE].astype(jnp.bfloat16))
        product = jnp.dot(
            chosen, jnp.concatenate(found, axis=1), preferred_element_type=jnp.float32
        )
        found = [product[:, p * LANE : (p + 1) * LANE].reshape(pairs, SUB, LANE) for p in (0, 1)]
        swapped = [pltpu.roll(x, SUB // 2, axis=1) for x in found]
        even = jnp.where(upper, found[0], swapped[1])
        odd = jnp.where(upper, swapped[0], found[1])
        result = jnp.stack([even, odd], axis=1).reshape(sources, slots, LANE)
        buffer[step] = result.astype(jnp.bfloat16)
        target = out_ref.at[:, :, step * LANE : (step + 1) * LANE]
        copies.append(pltpu.make_async_copy(buffer.at[step], target, sems.at[step]))
        copies[-1].start()
    for copy in copies:
        copy.wait()


def rows_kernel(capacity, parts, ids_ref, vectors_ref, out_ref):
    sources, slots = out_ref.shape[0], out_ref.shape[1]
    count, width = vectors_ref.shape
    piece = width // parts
    shape = (sources, slots, LANE)
    lane = lax.broadcasted_iota(jnp.int32, shape, 2)
    own = jnp.where(lane == lax.broadcasted_iota(jnp.int32, shape, 1), ids_ref[...], 0)
    ids = jnp.sum(own, axis=2, keepdims=True).reshape(sources * slots, 1)
    pieces = []
    for block in range(count // LANE):
        lane = lax.broadcasted_iota(jnp.int32, (sources * slots, LANE), 1) + block * LANE
        pieces.append(jnp.where(ids == lane, 1.0, 0.0).astype(jnp.bfloat16))
    chosen = jnp.concatenate(pieces, axis=1)
    slot = lax.broadcasted_iota(jnp.int32, (sources * slots, piece), 0) % slots
    result = None
    for part in range(parts):
        vectors = vectors_ref[:, part * piece : (part + 1) * piece].astype(jnp.bfloat16)
        found = jnp.dot(chosen, vectors, preferred_element_type=jnp.float32)
        result = found if part == 0 else jnp.where(slot >= part * capacity, found, result)
    out_ref[...] = result.reshape(sources, slots, piece).astype(jnp.bfloat16)


def final_kernel(capacity, parts, owner_ref, row_ref, queries_ref, rows_ref, out_ref):
    owners, slots, piece = rows_ref.shape
    q_dev, cands = out_ref.shape
    rows = rows_ref[...].reshape(owners * slots, piece)
    total = None
    for part in range(parts):
        x = queries_ref[:, part * piece : (part + 1) * piece]
        stacked = jnp.concatenate(split3(x), axis=0)
        product = lax.dot_general(
            stacked, rows, (((1,), (1,)), ((), ())), preferred_element_type=jnp.float32
        )
        scores = product[:q_dev] + product[q_dev : 2 * q_dev] + product[2 * q_dev :]
        if part:
            width = scores.shape[1]
            scores = pltpu.roll(scores, width - part * capacity, axis=1)
        total = scores if part == 0 else total + scores
    owner = owner_ref[...]
    padded = jnp.concatenate([owner, jnp.zeros((q_dev, LANE - cands), jnp.int32)], axis=1)
    rank = before(owner_table(owner, row_ref[...], owners))
    place = padded * slots + pick_wide(rank, padded)
    out_ref[...] = pick_wide(total, place)[:, :cands]


def join_kernel(*refs):
    rows = refs[0].shape[0]
    for n, ref in enumerate(refs[:-1]):
        refs[-1][n * rows : (n + 1) * rows] = ref[...]


def lists_kernel(lists, probes_ref, out_ref):
    total = probes_ref.shape[1]
    width = out_ref.shape[1]
    shard = lax.axis_index("shard")
    wanted = shard * lists + lax.broadcasted_iota(jnp.int32, (lists, total), 0)
    hit = jnp.zeros((lists, total), jnp.int32)
    for p in range(probes_ref.shape[0]):
        hit = jnp.where(probes_ref[p : p + 1, :] == wanted, 1, hit)
    upto = lax.broadcasted_iota(jnp.int32, (total, total), 0) >= lax.broadcasted_iota(
        jnp.int32, (total, total), 1
    )
    running = lax.dot_general(
        upto.astype(jnp.float32).astype(jnp.bfloat16),
        hit.astype(jnp.float32).astype(jnp.bfloat16),
        (((1,), (1,)), ((), ())),
        preferred_element_type=jnp.float32,
    )
    rank = lax.broadcasted_iota(jnp.int32, (total, width), 1).astype(jnp.float32)
    position = lax.broadcasted_iota(jnp.int32, (lists, total), 1)
    last = jnp.max(jnp.where(hit > 0, position, 0), axis=1, keepdims=True)
    counts = jnp.sum(hit, axis=1, keepdims=True)
    found = []
    for n in range(lists):
        passed = jnp.where(running[:, n : n + 1] <= rank, 1.0, 0.0)
        found.append(jnp.sum(passed, axis=0, keepdims=True))
    found = jnp.concatenate(found, axis=0).astype(jnp.int32)
    place = lax.broadcasted_iota(jnp.int32, (lists, width), 1)
    found = jnp.where(place < counts, found, last)
    found = jnp.where(place == width - 1, counts, found)
    out_ref[...] = found


def pq_kernel(q_dev, pieces, unroll, lists_hbm, codebook_ref, wide_codes, *refs):
    number = len(pieces)
    chunk_refs, (out_ref, queries, spread, table, codes, lists_s, sems) = (
        refs[:number],
        refs[number:],
    )
    lists, subs, entries = codes.shape
    total = queries.shape[0]
    centres = codebook_ref.shape[1]
    rows = 2 * SUB
    blocks = subs // rows
    shard = lax.axis_index("shard")

    send = pltpu.make_async_copy(lists_hbm, lists_s, sems.at[1])
    send.start()

    for (offset, begin, size), ref in zip(pieces, chunk_refs):
        start = 0 if offset is None else jnp.bitwise_xor(shard, offset) * q_dev
        queries[pl.ds(pl.multiple_of(start, q_dev), size), :] = ref[begin : begin + size, :]

    out_ref[...] = jnp.zeros(out_ref.shape, jnp.float32)

    half = LANE // 2
    lane = lax.broadcasted_iota(jnp.int32, (total, LANE), 1)
    inside = lax.broadcasted_iota(jnp.int32, (SUB, LANE), 1) % half // (half // SUB)
    own = jnp.where(inside == lax.broadcasted_iota(jnp.int32, (SUB, LANE), 0), 1.0, 0.0)

    def columns(k, carry):
        x = queries[:, pl.ds(pl.multiple_of(k * LANE, LANE), LANE)]
        swapped = pltpu.roll(x, half, axis=1)
        products = []
        for side in range(2):
            wide = jnp.where((lane < half) == (side == 0), x, swapped)
            high = wide.astype(jnp.bfloat16).astype(jnp.float32)
            spread[0] = high
            spread[1] = wide - high
            terms = []
            for term in range(2):
                lines = [
                    spread[term, pl.ds(q, SUB, stride=0), :] * own for q in range(total)
                ]
                terms.append(jnp.concatenate(lines, axis=0).astype(jnp.bfloat16))
            c = codebook_ref[pl.ds(pl.multiple_of(k * LANE + side * half, half), half), :]
            c_high = c.astype(jnp.bfloat16)
            c_low = (c - c_high.astype(jnp.float32)).astype(jnp.bfloat16)
            weights = jnp.concatenate([c_high, c_low, c_high, c_low], axis=0)
            product = jnp.dot(
                jnp.concatenate(terms, axis=1), weights, preferred_element_type=jnp.float32
            )
            products.append(product.reshape(total, SUB, centres))
        table[:, k] = jnp.concatenate(products, axis=1).astype(jnp.bfloat16)
        return carry

    lax.fori_loop(0, blocks, columns, 0)
    for n in range(lists):
        codes[n] = wide_codes[n].astype(jnp.int16)
    send.wait()
    halves = entries // LANE
    width = lists_s.shape[1]

    def emit(n, chosen, sums):
        for u in range(unroll):
            line = [
                jnp.sum(s, axis=0, keepdims=True) for s in sums[u * halves : (u + 1) * halves]
            ]
            out_ref[n, pl.ds(chosen[u], 1), :] = jnp.concatenate(line, axis=1)

    def one_list(n, carry):
        count = lists_s[n, width - 1]

        def some(step, inner):
            chosen = tuple(lists_s[n, step * unroll + u] for u in range(unroll))
            sums = [None] * (unroll * halves)
            for i in range(blocks):
                for h in range(halves):
                    code = codes[n, i * rows : (i + 1) * rows, h * LANE : (h + 1) * LANE]
                    low = jnp.bitwise_and(code, jnp.int16(LANE - 1))
                    for u in range(unroll):
                        value = pick(table[chosen[u], i, :, 0:LANE], low)
                        for part in range(1, centres // LANE):
                            other = pick(
                                table[chosen[u], i, :, part * LANE : (part + 1) * LANE], low
                            )
                            value = jnp.where(code >= jnp.int16(part * LANE), other, value)
                        value = value.astype(jnp.float32)
                        value = value[:SUB] + value[SUB:]
                        at = u * halves + h
                        sums[at] = value if i == 0 else sums[at] + value
                if i == 1:
                    emit(*inner)
            return n, chosen, tuple(sums)

        return lax.fori_loop(0, (count + unroll - 1) // unroll, some, carry)

    first = (
        jnp.int32(0),
        (jnp.int32(0),) * unroll,
        (jnp.zeros((SUB, LANE), jnp.float32),) * (unroll * halves),
    )
    emit(*lax.fori_loop(0, lists, one_list, first))


def whole(memory=pltpu.VMEM):
    return pl.BlockSpec(memory_space=memory)


def per_device(queries, codebook, pq_codes, probes, vectors, cand_owner, cand_row):
    shards = lax.axis_size("shard")
    owners = lax.axis_size("group") * shards
    q_dev, width = queries.shape
    cands = cand_owner.shape[1]
    subs, centres, dims = codebook.shape
    lists, _, entries = pq_codes.shape
    total = q_dev * shards
    capacity, parts = layout_of(q_dev * cands, owners, width)
    unroll = 8

    ids = pl.pallas_call(
        lambda *refs: ids_kernel(capacity, parts, *refs),
        out_shape=jax.ShapeDtypeStruct((owners, 1, LANE), jnp.int32),
        in_specs=[whole()] * 2,
        out_specs=whole(),
        name="ids",
        cost_estimate=pl.CostEstimate(flops=10**9, bytes_accessed=6 << 20, transcendentals=0),
    )(cand_owner, cand_row)
    list_width = -(-(total + unroll + 1) // LANE) * LANE
    grouping = pl.pallas_call(
        lambda *refs: lists_kernel(lists, *refs),
        out_shape=jax.ShapeDtypeStruct((lists, list_width), jnp.int32),
        in_specs=[whole()],
        out_specs=whole(),
        name="groups",
        compiler_params=pltpu.CompilerParams(vmem_limit_bytes=4 << 20),
        cost_estimate=pl.CostEstimate(flops=10**9, bytes_accessed=12 << 20, transcendentals=0),
    )
    groups = grouping(probes.T)
    own, groups = lax.optimization_barrier((queries, groups))
    asked = lax.all_to_all(ids, AXES, split_axis=0, concat_axis=0, tiled=True)

    near = [queries]
    if shards == 8:
        near += [
            lax.ppermute(own, "shard", [(i, i ^ k) for i in range(shards)])
            for k in range(2, shards, 2)
        ]
    else:
        gathered = lax.all_gather(queries, "shard", axis=0, tiled=True)

    paired = capacity * 2 == SUB and parts == 2 and owners % 2 == 0
    piece = width // parts
    kernel, scratch = lambda *refs: rows_kernel(capacity, parts, *refs), []
    if paired:
        kernel = paired_rows_kernel
        scratch = [
            pltpu.VMEM((piece // LANE, owners, SUB, LANE), jnp.bfloat16),
            pltpu.SemaphoreType.DMA((piece // LANE,)),
        ]
    rows = pl.pallas_call(
        kernel,
        out_shape=jax.ShapeDtypeStruct((owners, SUB, piece), jnp.bfloat16),
        in_specs=[whole()] * 2,
        out_specs=whole(pl.ANY) if paired else whole(),
        scratch_shapes=scratch,
        name="rows",
        compiler_params=pltpu.CompilerParams(vmem_limit_bytes=16 << 20),
        cost_estimate=pl.CostEstimate(flops=10**9, bytes_accessed=4 << 20, transcendentals=0),
    )(asked, vectors)
    returned = lax.all_to_all(rows, AXES, split_axis=0, concat_axis=0, tiled=True)
    pieces, chunks = [], []
    if shards == 8:
        joined = pl.pallas_call(
            join_kernel,
            out_shape=jax.ShapeDtypeStruct((len(near) * q_dev, width), jnp.float32),
            in_specs=[whole()] * len(near),
            out_specs=whole(),
            name="join",
            compiler_params=pltpu.CompilerParams(vmem_limit_bytes=4 << 20),
            cost_estimate=pl.CostEstimate(flops=10**9, bytes_accessed=16 << 20, transcendentals=0),
        )(*near)
        other = lax.ppermute(joined, "shard", [(i, i ^ 1) for i in range(shards)])
        for side, chunk in enumerate((joined, other)):
            for n in range(len(near)):
                chunks.append(chunk)
                pieces.append((2 * n ^ side, n * q_dev, q_dev))
    else:
        pieces.append((None, 0, total))
        chunks.append(gathered)

    pq = pl.pallas_call(
        lambda *refs: pq_kernel(q_dev, pieces, unroll, *refs),
        out_shape=jax.ShapeDtypeStruct((lists, total, entries), jnp.float32),
        in_specs=[whole(pl.ANY)] + [whole()] * 2 + [whole()] * len(chunks),
        out_specs=whole(),
        scratch_shapes=[
            pltpu.VMEM((total, width), jnp.float32),
            pltpu.VMEM((2, total, LANE), jnp.float32),
            pltpu.VMEM((total, subs // SUB // 2, 2 * SUB, centres), jnp.bfloat16),
            pltpu.VMEM((lists, subs, entries), jnp.int16),
            pltpu.SMEM((lists, list_width), jnp.int32),
            pltpu.SemaphoreType.DMA((3,)),
        ],
        name="pq",
        compiler_params=pltpu.CompilerParams(
            vmem_limit_bytes=14300000
        ),
        cost_estimate=pl.CostEstimate(
            flops=10**10, bytes_accessed=30 << 20, transcendentals=0
        ),
    )(
        groups,
        codebook.transpose(0, 2, 1).reshape(subs * dims, centres),
        pq_codes,
        *chunks,
    )

    rerank = pl.pallas_call(
        lambda *refs: final_kernel(capacity, parts, *refs),
        out_shape=jax.ShapeDtypeStruct((q_dev, cands), jnp.float32),
        in_specs=[whole()] * 4,
        out_specs=whole(),
        name="final",
        compiler_params=pltpu.CompilerParams(vmem_limit_bytes=8 << 20),
    )(cand_owner, cand_row, queries, returned)
    return pq.transpose(0, 2, 1), rerank


def solution(mesh):
    in_specs = (
        P(AXES, None),
        P(),
        P(AXES, None, None),
        P("group", None),
        P(AXES, None),
        P(AXES, None),
        P(AXES, None),
    )
    out_specs = (P(AXES, None, None), P(AXES, None))
    return jax.shard_map(
        per_device, mesh=mesh, in_specs=in_specs, out_specs=out_specs, check_vma=False
    )
```

```python
import jax
import jax.numpy as jnp
from jax import lax
from jax.experimental import pallas as pl
from jax.experimental.pallas import tpu as pltpu
from jax.sharding import PartitionSpec as P


AXES = ("group", "shard")
SUB = 8
LANE = 128
GATHER = lax.GatherDimensionNumbers(
    offset_dims=(),
    collapsed_slice_dims=(1,),
    start_index_map=(1,),
    operand_batching_dims=(0,),
    start_indices_batching_dims=(0,),
)


def pick(table, index):
    return lax.gather(
        table, index[..., None], GATHER, (1, 1), mode=lax.GatherScatterMode.PROMISE_IN_BOUNDS
    )


def pick_wide(table, index):
    low = jnp.bitwise_and(index, LANE - 1)
    result = pick(table[:, :LANE], low)
    for part in range(1, table.shape[1] // LANE):
        found = pick(table[:, part * LANE : (part + 1) * LANE], low)
        result = jnp.where(index >= part * LANE, found, result)
    return result


def split3(x):
    high = x.astype(jnp.bfloat16)
    rest = x - high.astype(jnp.float32)
    middle = rest.astype(jnp.bfloat16)
    low = (rest - middle.astype(jnp.float32)).astype(jnp.bfloat16)
    return high, middle, low


def owner_table(owner, row, owners):
    q_dev, cands = owner.shape
    width = -(-owners // LANE) * LANE
    lane = lax.broadcasted_iota(jnp.int32, (q_dev, width), 1)
    table = jnp.full((q_dev, width), -1, jnp.int32)
    for c in range(cands):
        table = jnp.where(lane == owner[:, c : c + 1], row[:, c : c + 1], table)
    return table


def before(table):
    asked = (table >= 0).astype(jnp.int32)
    rows = [jnp.zeros_like(asked[0:1])]
    for q in range(1, table.shape[0]):
        rows.append(rows[-1] + asked[q - 1 : q])
    return jnp.concatenate(rows, axis=0)


def layout_of(pair_count, owners, width):
    capacity = max(2, pair_count // owners)
    parts = max(
        p for p in range(1, 9) if p == 1 or (p * capacity <= SUB and width % (p * LANE) == 0)
    )
    return capacity, parts


def ids_kernel(capacity, parts, owner_ref, row_ref, out_ref):
    owners = out_ref.shape[0]
    table = owner_table(owner_ref[...], row_ref[...], owners)
    rank = before(table)
    rows = []
    for s in range(capacity):
        rows.append(jnp.max(jnp.where(rank == s, table, -1), axis=0, keepdims=True))
    rows = rows * parts
    rows += [jnp.full_like(rows[0], -1)] * (SUB - len(rows))
    packed = jnp.concatenate(rows, axis=0)
    for block in range(packed.shape[1] // LANE):
        square = jnp.concatenate(
            [packed[:, block * LANE : (block + 1) * LANE]]
            + [jnp.zeros((LANE - SUB, LANE), jnp.int32)],
            axis=0,
        )
        count = min(LANE, owners - block * LANE)
        turned = square.T[:count]
        out_ref[block * LANE : block * LANE + count] = turned.reshape(count, 1, LANE)


def paired_rows_kernel(ids_ref, vectors_ref, out_ref, buffer, sems):
    sources, slots, piece = out_ref.shape
    count = vectors_ref.shape[0]
    pairs = sources // 2
    shape = (pairs, SUB, LANE)
    lane = lax.broadcasted_iota(jnp.int32, shape, 2)
    row = lax.broadcasted_iota(jnp.int32, shape, 1)
    ids = ids_ref[...].reshape(pairs, 2, 1, LANE)
    mine = jnp.where(row < SUB // 2, ids[:, 0], ids[:, 1])
    mine = jnp.where(lane == row % (SUB // 2), mine, 0)
    wanted = jnp.sum(mine, axis=2, keepdims=True).reshape(pairs * SUB, 1)
    chosen = []
    for block in range(count // LANE):
        lane = lax.broadcasted_iota(jnp.int32, (pairs * SUB, LANE), 1) + block * LANE
        chosen.append(jnp.where(wanted == lane, 1.0, 0.0).astype(jnp.bfloat16))
    chosen = jnp.concatenate(chosen, axis=1)
    upper = lax.broadcasted_iota(jnp.int32, (pairs, SUB, LANE), 1) < SUB // 2
    copies = []
    for step in range(piece // LANE):
        found = []
        for part in range(2):
            start = part * piece + step * LANE
            found.append(vectors_ref[:, start : start + LANE].astype(jnp.bfloat16))
        product = jnp.dot(
            chosen, jnp.concatenate(found, axis=1), preferred_element_type=jnp.float32
        )
        found = [product[:, p * LANE : (p + 1) * LANE].reshape(pairs, SUB, LANE) for p in (0, 1)]
        swapped = [pltpu.roll(x, SUB // 2, axis=1) for x in found]
        even = jnp.where(upper, found[0], swapped[1])
        odd = jnp.where(upper, swapped[0], found[1])
        result = jnp.stack([even, odd], axis=1).reshape(sources, slots, LANE)
        buffer[step] = result.astype(jnp.bfloat16)
        target = out_ref.at[:, :, step * LANE : (step + 1) * LANE]
        copies.append(pltpu.make_async_copy(buffer.at[step], target, sems.at[step]))
        copies[-1].start()
    for copy in copies:
        copy.wait()


def rows_kernel(capacity, parts, ids_ref, vectors_ref, out_ref):
    sources, slots = out_ref.shape[0], out_ref.shape[1]
    count, width = vectors_ref.shape
    piece = width // parts
    shape = (sources, slots, LANE)
    lane = lax.broadcasted_iota(jnp.int32, shape, 2)
    own = jnp.where(lane == lax.broadcasted_iota(jnp.int32, shape, 1), ids_ref[...], 0)
    ids = jnp.sum(own, axis=2, keepdims=True).reshape(sources * slots, 1)
    pieces = []
    for block in range(count // LANE):
        lane = lax.broadcasted_iota(jnp.int32, (sources * slots, LANE), 1) + block * LANE
        pieces.append(jnp.where(ids == lane, 1.0, 0.0).astype(jnp.bfloat16))
    chosen = jnp.concatenate(pieces, axis=1)
    slot = lax.broadcasted_iota(jnp.int32, (sources * slots, piece), 0) % slots
    result = None
    for part in range(parts):
        vectors = vectors_ref[:, part * piece : (part + 1) * piece].astype(jnp.bfloat16)
        found = jnp.dot(chosen, vectors, preferred_element_type=jnp.float32)
        result = found if part == 0 else jnp.where(slot >= part * capacity, found, result)
    out_ref[...] = result.reshape(sources, slots, piece).astype(jnp.bfloat16)


def final_kernel(capacity, parts, owner_ref, row_ref, queries_ref, rows_ref, out_ref):
    owners, slots, piece = rows_ref.shape
    q_dev, cands = out_ref.shape
    rows = rows_ref[...].reshape(owners * slots, piece)
    total = None
    for part in range(parts):
        x = queries_ref[:, part * piece : (part + 1) * piece]
        stacked = jnp.concatenate(split3(x), axis=0)
        product = lax.dot_general(
            stacked, rows, (((1,), (1,)), ((), ())), preferred_element_type=jnp.float32
        )
        scores = product[:q_dev] + product[q_dev : 2 * q_dev] + product[2 * q_dev :]
        if part:
            width = scores.shape[1]
            scores = pltpu.roll(scores, width - part * capacity, axis=1)
        total = scores if part == 0 else total + scores
    owner = owner_ref[...]
    padded = jnp.concatenate([owner, jnp.zeros((q_dev, LANE - cands), jnp.int32)], axis=1)
    rank = before(owner_table(owner, row_ref[...], owners))
    place = padded * slots + pick_wide(rank, padded)
    out_ref[...] = pick_wide(total, place)[:, :cands]


def join_kernel(*refs):
    rows = refs[0].shape[0]
    for n, ref in enumerate(refs[:-1]):
        refs[-1][n * rows : (n + 1) * rows] = ref[...]


def lists_kernel(lists, probes_ref, out_ref):
    total = probes_ref.shape[1]
    width = out_ref.shape[1]
    shard = lax.axis_index("shard")
    wanted = shard * lists + lax.broadcasted_iota(jnp.int32, (lists, total), 0)
    hit = jnp.zeros((lists, total), jnp.int32)
    for p in range(probes_ref.shape[0]):
        hit = jnp.where(probes_ref[p : p + 1, :] == wanted, 1, hit)
    upto = lax.broadcasted_iota(jnp.int32, (total, total), 0) >= lax.broadcasted_iota(
        jnp.int32, (total, total), 1
    )
    running = lax.dot_general(
        upto.astype(jnp.float32).astype(jnp.bfloat16),
        hit.astype(jnp.float32).astype(jnp.bfloat16),
        (((1,), (1,)), ((), ())),
        preferred_element_type=jnp.float32,
    )
    rank = lax.broadcasted_iota(jnp.int32, (total, width), 1).astype(jnp.float32)
    position = lax.broadcasted_iota(jnp.int32, (lists, total), 1)
    last = jnp.max(jnp.where(hit > 0, position, 0), axis=1, keepdims=True)
    counts = jnp.sum(hit, axis=1, keepdims=True)
    found = []
    for n in range(lists):
        passed = jnp.where(running[:, n : n + 1] <= rank, 1.0, 0.0)
        found.append(jnp.sum(passed, axis=0, keepdims=True))
    found = jnp.concatenate(found, axis=0).astype(jnp.int32)
    place = lax.broadcasted_iota(jnp.int32, (lists, width), 1)
    found = jnp.where(place < counts, found, last)
    found = jnp.where(place == width - 1, counts, found)
    out_ref[...] = found


def pq_kernel(q_dev, pieces, unroll, lists_hbm, codebook_ref, wide_codes, *refs):
    number = len(pieces)
    chunk_refs, (out_ref, queries, spread, table, codes, lists_s, sems) = (
        refs[:number],
        refs[number:],
    )
    lists, subs, entries = codes.shape
    total = queries.shape[0]
    centres = codebook_ref.shape[1]
    rows = 2 * SUB
    blocks = subs // rows
    shard = lax.axis_index("shard")

    send = pltpu.make_async_copy(lists_hbm, lists_s, sems.at[1])
    send.start()

    for (offset, begin, size), ref in zip(pieces, chunk_refs):
        start = 0 if offset is None else jnp.bitwise_xor(shard, offset) * q_dev
        queries[pl.ds(pl.multiple_of(start, q_dev), size), :] = ref[begin : begin + size, :]

    out_ref[...] = jnp.zeros(out_ref.shape, jnp.float32)

    half = LANE // 2
    lane = lax.broadcasted_iota(jnp.int32, (total, LANE), 1)
    inside = lax.broadcasted_iota(jnp.int32, (SUB, LANE), 1) % half // (half // SUB)
    own = jnp.where(inside == lax.broadcasted_iota(jnp.int32, (SUB, LANE), 0), 1.0, 0.0)

    def columns(k, carry):
        x = queries[:, pl.ds(pl.multiple_of(k * LANE, LANE), LANE)]
        swapped = pltpu.roll(x, half, axis=1)
        products = []
        for side in range(2):
            wide = jnp.where((lane < half) == (side == 0), x, swapped)
            high = wide.astype(jnp.bfloat16).astype(jnp.float32)
            spread[0] = high
            spread[1] = wide - high
            terms = []
            for term in range(2):
                lines = [
                    spread[term, pl.ds(q, SUB, stride=0), :] * own for q in range(total)
                ]
                terms.append(jnp.concatenate(lines, axis=0).astype(jnp.bfloat16))
            c = codebook_ref[pl.ds(pl.multiple_of(k * LANE + side * half, half), half), :]
            c_high = c.astype(jnp.bfloat16)
            c_low = (c - c_high.astype(jnp.float32)).astype(jnp.bfloat16)
            weights = jnp.concatenate([c_high, c_low, c_high, c_low], axis=0)
            product = jnp.dot(
                jnp.concatenate(terms, axis=1), weights, preferred_element_type=jnp.float32
            )
            products.append(product.reshape(total, SUB, centres))
        table[:, k] = jnp.concatenate(products, axis=1).astype(jnp.bfloat16)
        return carry

    lax.fori_loop(0, blocks, columns, 0)
    for n in range(lists):
        codes[n] = wide_codes[n].astype(jnp.int16)
    send.wait()
    halves = entries // LANE
    width = lists_s.shape[1]

    def emit(n, chosen, sums):
        for u in range(unroll):
            line = [
                jnp.sum(s, axis=0, keepdims=True) for s in sums[u * halves : (u + 1) * halves]
            ]
            out_ref[n, pl.ds(chosen[u], 1), :] = jnp.concatenate(line, axis=1)

    def group(n, begin, size, inner):
        chosen = [lists_s[n, begin + u] for u in range(size)]
        sums = [None] * (size * halves)
        for i in range(blocks):
            for h in range(halves):
                code = codes[n, i * rows : (i + 1) * rows, h * LANE : (h + 1) * LANE]
                low = jnp.bitwise_and(code, jnp.int16(LANE - 1))
                for u in range(size):
                    value = pick(table[chosen[u], i, :, 0:LANE], low)
                    for part in range(1, centres // LANE):
                        other = pick(table[chosen[u], i, :, part * LANE : (part + 1) * LANE], low)
                        value = jnp.where(code >= jnp.int16(part * LANE), other, value)
                    value = value.astype(jnp.float32)
                    value = value[:SUB] + value[SUB:]
                    at = u * halves + h
                    sums[at] = value if i == 0 else sums[at] + value
            if i == 1:
                emit(*inner)
        chosen += chosen[-1:] * (unroll - size)
        sums += sums[-halves:] * (unroll - size)
        return n, tuple(chosen), tuple(sums)

    short = unroll // 2

    def one_list(n, carry):
        count = lists_s[n, width - 1]
        steps = (count + unroll - short - 1) // unroll
        carry = lax.fori_loop(
            0, steps, lambda step, inner: group(n, step * unroll, unroll, inner), carry
        )
        left = (count - steps * unroll > 0).astype(jnp.int32)
        return lax.fori_loop(
            0, left, lambda step, inner: group(n, steps * unroll, short, inner), carry
        )

    first = (
        jnp.int32(0),
        (jnp.int32(0),) * unroll,
        (jnp.zeros((SUB, LANE), jnp.float32),) * (unroll * halves),
    )
    emit(*lax.fori_loop(0, lists, one_list, first))


def whole(memory=pltpu.VMEM):
    return pl.BlockSpec(memory_space=memory)


def per_device(queries, codebook, pq_codes, probes, vectors, cand_owner, cand_row):
    shards = lax.axis_size("shard")
    owners = lax.axis_size("group") * shards
    q_dev, width = queries.shape
    cands = cand_owner.shape[1]
    subs, centres, dims = codebook.shape
    lists, _, entries = pq_codes.shape
    total = q_dev * shards
    capacity, parts = layout_of(q_dev * cands, owners, width)
    unroll = 8

    ids = pl.pallas_call(
        lambda *refs: ids_kernel(capacity, parts, *refs),
        out_shape=jax.ShapeDtypeStruct((owners, 1, LANE), jnp.int32),
        in_specs=[whole()] * 2,
        out_specs=whole(),
        name="ids",
        cost_estimate=pl.CostEstimate(flops=10**9, bytes_accessed=6 << 20, transcendentals=0),
    )(cand_owner, cand_row)
    list_width = -(-(total + unroll + 1) // LANE) * LANE
    grouping = pl.pallas_call(
        lambda *refs: lists_kernel(lists, *refs),
        out_shape=jax.ShapeDtypeStruct((lists, list_width), jnp.int32),
        in_specs=[whole()],
        out_specs=whole(),
        name="groups",
        compiler_params=pltpu.CompilerParams(vmem_limit_bytes=4 << 20),
        cost_estimate=pl.CostEstimate(flops=10**9, bytes_accessed=12 << 20, transcendentals=0),
    )
    groups = grouping(probes.T)
    own, groups = lax.optimization_barrier((queries, groups))
    asked = lax.all_to_all(ids, AXES, split_axis=0, concat_axis=0, tiled=True)

    near = [queries]
    if shards == 8:
        near += [
            lax.ppermute(own, "shard", [(i, i ^ k) for i in range(shards)])
            for k in range(2, shards, 2)
        ]
    else:
        gathered = lax.all_gather(queries, "shard", axis=0, tiled=True)

    paired = capacity * 2 == SUB and parts == 2 and owners % 2 == 0
    piece = width // parts
    kernel, scratch = lambda *refs: rows_kernel(capacity, parts, *refs), []
    if paired:
        kernel = paired_rows_kernel
        scratch = [
            pltpu.VMEM((piece // LANE, owners, SUB, LANE), jnp.bfloat16),
            pltpu.SemaphoreType.DMA((piece // LANE,)),
        ]
    rows = pl.pallas_call(
        kernel,
        out_shape=jax.ShapeDtypeStruct((owners, SUB, piece), jnp.bfloat16),
        in_specs=[whole()] * 2,
        out_specs=whole(pl.ANY) if paired else whole(),
        scratch_shapes=scratch,
        name="rows",
        compiler_params=pltpu.CompilerParams(vmem_limit_bytes=16 << 20),
        cost_estimate=pl.CostEstimate(flops=10**9, bytes_accessed=4 << 20, transcendentals=0),
    )(asked, vectors)
    returned = lax.all_to_all(rows, AXES, split_axis=0, concat_axis=0, tiled=True)
    pieces, chunks = [], []
    if shards == 8:
        joined = pl.pallas_call(
            join_kernel,
            out_shape=jax.ShapeDtypeStruct((len(near) * q_dev, width), jnp.float32),
            in_specs=[whole()] * len(near),
            out_specs=whole(),
            name="join",
            compiler_params=pltpu.CompilerParams(vmem_limit_bytes=4 << 20),
            cost_estimate=pl.CostEstimate(flops=10**9, bytes_accessed=16 << 20, transcendentals=0),
        )(*near)
        other = lax.ppermute(joined, "shard", [(i, i ^ 1) for i in range(shards)])
        for side, chunk in enumerate((joined, other)):
            for n in range(len(near)):
                chunks.append(chunk)
                pieces.append((2 * n ^ side, n * q_dev, q_dev))
    else:
        pieces.append((None, 0, total))
        chunks.append(gathered)

    pq = pl.pallas_call(
        lambda *refs: pq_kernel(q_dev, pieces, unroll, *refs),
        out_shape=jax.ShapeDtypeStruct((lists, total, entries), jnp.float32),
        in_specs=[whole(pl.ANY)] + [whole()] * 2 + [whole()] * len(chunks),
        out_specs=whole(),
        scratch_shapes=[
            pltpu.VMEM((total, width), jnp.float32),
            pltpu.VMEM((2, total, LANE), jnp.float32),
            pltpu.VMEM((total, subs // SUB // 2, 2 * SUB, centres), jnp.bfloat16),
            pltpu.VMEM((lists, subs, entries), jnp.int16),
            pltpu.SMEM((lists, list_width), jnp.int32),
            pltpu.SemaphoreType.DMA((3,)),
        ],
        name="pq",
        compiler_params=pltpu.CompilerParams(
            vmem_limit_bytes=14300000
        ),
        cost_estimate=pl.CostEstimate(
            flops=10**10, bytes_accessed=30 << 20, transcendentals=0
        ),
    )(
        groups,
        codebook.transpose(0, 2, 1).reshape(subs * dims, centres),
        pq_codes,
        *chunks,
    )

    rerank = pl.pallas_call(
        lambda *refs: final_kernel(capacity, parts, *refs),
        out_shape=jax.ShapeDtypeStruct((q_dev, cands), jnp.float32),
        in_specs=[whole()] * 4,
        out_specs=whole(),
        name="final",
        compiler_params=pltpu.CompilerParams(vmem_limit_bytes=8 << 20),
    )(cand_owner, cand_row, queries, returned)
    return pq.transpose(0, 2, 1), rerank


def solution(mesh):
    in_specs = (
        P(AXES, None),
        P(),
        P(AXES, None, None),
        P("group", None),
        P(AXES, None),
        P(AXES, None),
        P(AXES, None),
    )
    out_specs = (P(AXES, None, None), P(AXES, None))
    return jax.shard_map(
        per_device, mesh=mesh, in_specs=in_specs, out_specs=out_specs, check_vma=False
    )
```

```python
import jax
import jax.numpy as jnp
from jax import lax
from jax.experimental import pallas as pl
from jax.experimental.pallas import tpu as pltpu
from jax.sharding import PartitionSpec as P


AXES = ("group", "shard")
SUB = 8
LANE = 128
GATHER = lax.GatherDimensionNumbers(
    offset_dims=(),
    collapsed_slice_dims=(1,),
    start_index_map=(1,),
    operand_batching_dims=(0,),
    start_indices_batching_dims=(0,),
)


def pick(table, index):
    return lax.gather(
        table, index[..., None], GATHER, (1, 1), mode=lax.GatherScatterMode.PROMISE_IN_BOUNDS
    )


def pick_wide(table, index):
    low = jnp.bitwise_and(index, LANE - 1)
    result = pick(table[:, :LANE], low)
    for part in range(1, table.shape[1] // LANE):
        found = pick(table[:, part * LANE : (part + 1) * LANE], low)
        result = jnp.where(index >= part * LANE, found, result)
    return result


def split3(x):
    high = x.astype(jnp.bfloat16)
    rest = x - high.astype(jnp.float32)
    middle = rest.astype(jnp.bfloat16)
    low = (rest - middle.astype(jnp.float32)).astype(jnp.bfloat16)
    return high, middle, low


def owner_table(owner, row, owners):
    q_dev, cands = owner.shape
    width = -(-owners // LANE) * LANE
    lane = lax.broadcasted_iota(jnp.int32, (q_dev, width), 1)
    table = jnp.full((q_dev, width), -1, jnp.int32)
    for c in range(cands):
        table = jnp.where(lane == owner[:, c : c + 1], row[:, c : c + 1], table)
    return table


def before(table):
    asked = (table >= 0).astype(jnp.int32)
    rows = [jnp.zeros_like(asked[0:1])]
    for q in range(1, table.shape[0]):
        rows.append(rows[-1] + asked[q - 1 : q])
    return jnp.concatenate(rows, axis=0)


def layout_of(pair_count, owners, width):
    capacity = max(2, pair_count // owners)
    parts = max(
        p for p in range(1, 9) if p == 1 or (p * capacity <= SUB and width % (p * LANE) == 0)
    )
    return capacity, parts


def ids_kernel(capacity, parts, owner_ref, row_ref, out_ref):
    owners = out_ref.shape[0]
    table = owner_table(owner_ref[...], row_ref[...], owners)
    rank = before(table)
    rows = []
    for s in range(capacity):
        rows.append(jnp.max(jnp.where(rank == s, table, -1), axis=0, keepdims=True))
    rows = rows * parts
    rows += [jnp.full_like(rows[0], -1)] * (SUB - len(rows))
    packed = jnp.concatenate(rows, axis=0)
    for block in range(packed.shape[1] // LANE):
        square = jnp.concatenate(
            [packed[:, block * LANE : (block + 1) * LANE]]
            + [jnp.zeros((LANE - SUB, LANE), jnp.int32)],
            axis=0,
        )
        count = min(LANE, owners - block * LANE)
        turned = square.T[:count]
        out_ref[block * LANE : block * LANE + count] = turned.reshape(count, 1, LANE)


def paired_rows_kernel(ids_ref, vectors_ref, out_ref, buffer, sems):
    sources, slots, piece = out_ref.shape
    count = vectors_ref.shape[0]
    pairs = sources // 2
    shape = (pairs, SUB, LANE)
    lane = lax.broadcasted_iota(jnp.int32, shape, 2)
    row = lax.broadcasted_iota(jnp.int32, shape, 1)
    ids = ids_ref[...].reshape(pairs, 2, 1, LANE)
    mine = jnp.where(row < SUB // 2, ids[:, 0], ids[:, 1])
    mine = jnp.where(lane == row % (SUB // 2), mine, 0)
    wanted = jnp.sum(mine, axis=2, keepdims=True).reshape(pairs * SUB, 1)
    chosen = []
    for block in range(count // LANE):
        lane = lax.broadcasted_iota(jnp.int32, (pairs * SUB, LANE), 1) + block * LANE
        chosen.append(jnp.where(wanted == lane, 1.0, 0.0).astype(jnp.bfloat16))
    chosen = jnp.concatenate(chosen, axis=1)
    upper = lax.broadcasted_iota(jnp.int32, (pairs, SUB, LANE), 1) < SUB // 2
    copies = []
    for step in range(piece // LANE):
        found = []
        for part in range(2):
            start = part * piece + step * LANE
            found.append(vectors_ref[:, start : start + LANE].astype(jnp.bfloat16))
        product = jnp.dot(
            chosen, jnp.concatenate(found, axis=1), preferred_element_type=jnp.float32
        )
        found = [product[:, p * LANE : (p + 1) * LANE].reshape(pairs, SUB, LANE) for p in (0, 1)]
        swapped = [pltpu.roll(x, SUB // 2, axis=1) for x in found]
        even = jnp.where(upper, found[0], swapped[1])
        odd = jnp.where(upper, swapped[0], found[1])
        result = jnp.stack([even, odd], axis=1).reshape(sources, slots, LANE)
        buffer[step] = result.astype(jnp.bfloat16)
        target = out_ref.at[:, :, step * LANE : (step + 1) * LANE]
        copies.append(pltpu.make_async_copy(buffer.at[step], target, sems.at[step]))
        copies[-1].start()
    for copy in copies:
        copy.wait()


def rows_kernel(capacity, parts, ids_ref, vectors_ref, out_ref):
    sources, slots = out_ref.shape[0], out_ref.shape[1]
    count, width = vectors_ref.shape
    piece = width // parts
    shape = (sources, slots, LANE)
    lane = lax.broadcasted_iota(jnp.int32, shape, 2)
    own = jnp.where(lane == lax.broadcasted_iota(jnp.int32, shape, 1), ids_ref[...], 0)
    ids = jnp.sum(own, axis=2, keepdims=True).reshape(sources * slots, 1)
    pieces = []
    for block in range(count // LANE):
        lane = lax.broadcasted_iota(jnp.int32, (sources * slots, LANE), 1) + block * LANE
        pieces.append(jnp.where(ids == lane, 1.0, 0.0).astype(jnp.bfloat16))
    chosen = jnp.concatenate(pieces, axis=1)
    slot = lax.broadcasted_iota(jnp.int32, (sources * slots, piece), 0) % slots
    result = None
    for part in range(parts):
        vectors = vectors_ref[:, part * piece : (part + 1) * piece].astype(jnp.bfloat16)
        found = jnp.dot(chosen, vectors, preferred_element_type=jnp.float32)
        result = found if part == 0 else jnp.where(slot >= part * capacity, found, result)
    out_ref[...] = result.reshape(sources, slots, piece).astype(jnp.bfloat16)


def final_kernel(capacity, parts, place_ref, queries_ref, rows_ref, out_ref):
    owners, slots, piece = rows_ref.shape
    q_dev, cands = out_ref.shape
    rows = rows_ref[...].reshape(owners * slots, piece)
    total = None
    for part in range(parts):
        x = queries_ref[:, part * piece : (part + 1) * piece]
        stacked = jnp.concatenate(split3(x), axis=0)
        product = lax.dot_general(
            stacked, rows, (((1,), (1,)), ((), ())), preferred_element_type=jnp.float32
        )
        scores = product[:q_dev] + product[q_dev : 2 * q_dev] + product[2 * q_dev :]
        if part:
            width = scores.shape[1]
            scores = pltpu.roll(scores, width - part * capacity, axis=1)
        total = scores if part == 0 else total + scores
    place = place_ref[...]
    out_ref[...] = pick_wide(total, place)[:, :cands]


def join_kernel(*refs):
    rows = refs[0].shape[0]
    for n, ref in enumerate(refs[:-1]):
        refs[-1][n * rows : (n + 1) * rows] = ref[...]


def lists_kernel(lists, owners, probes_ref, owner_ref, row_ref, out_ref, place_ref):
    q_dev, cands = owner_ref.shape
    slots = SUB
    owner = owner_ref[...]
    padded = jnp.concatenate([owner, jnp.zeros((q_dev, LANE - cands), jnp.int32)], axis=1)
    rank = before(owner_table(owner, row_ref[...], owners))
    place_ref[...] = padded * slots + pick_wide(rank, padded)
    total = probes_ref.shape[1]
    width = out_ref.shape[1]
    shard = lax.axis_index("shard")
    wanted = shard * lists + lax.broadcasted_iota(jnp.int32, (lists, total), 0)
    hit = jnp.zeros((lists, total), jnp.int32)
    for p in range(probes_ref.shape[0]):
        hit = jnp.where(probes_ref[p : p + 1, :] == wanted, 1, hit)
    upto = lax.broadcasted_iota(jnp.int32, (total, total), 0) >= lax.broadcasted_iota(
        jnp.int32, (total, total), 1
    )
    running = lax.dot_general(
        upto.astype(jnp.float32).astype(jnp.bfloat16),
        hit.astype(jnp.float32).astype(jnp.bfloat16),
        (((1,), (1,)), ((), ())),
        preferred_element_type=jnp.float32,
    )
    rank = lax.broadcasted_iota(jnp.int32, (total, width), 1).astype(jnp.float32)
    position = lax.broadcasted_iota(jnp.int32, (lists, total), 1)
    last = jnp.max(jnp.where(hit > 0, position, 0), axis=1, keepdims=True)
    counts = jnp.sum(hit, axis=1, keepdims=True)
    found = []
    for n in range(lists):
        passed = jnp.where(running[:, n : n + 1] <= rank, 1.0, 0.0)
        found.append(jnp.sum(passed, axis=0, keepdims=True))
    found = jnp.concatenate(found, axis=0).astype(jnp.int32)
    place = lax.broadcasted_iota(jnp.int32, (lists, width), 1)
    found = jnp.where(place < counts, found, last)
    found = jnp.where(place == width - 1, counts, found)
    out_ref[...] = found


def pq_kernel(q_dev, pieces, unroll, lists_hbm, codebook_ref, wide_codes, *refs):
    number = len(pieces)
    chunk_refs, (out_ref, queries, spread, table, codes, lists_s, sems) = (
        refs[:number],
        refs[number:],
    )
    lists, subs, entries = codes.shape
    total = queries.shape[0]
    centres = codebook_ref.shape[1]
    rows = 2 * SUB
    blocks = subs // rows
    shard = lax.axis_index("shard")

    send = pltpu.make_async_copy(lists_hbm, lists_s, sems.at[1])
    send.start()

    for (offset, begin, size), ref in zip(pieces, chunk_refs):
        start = 0 if offset is None else jnp.bitwise_xor(shard, offset) * q_dev
        queries[pl.ds(pl.multiple_of(start, q_dev), size), :] = ref[begin : begin + size, :]

    out_ref[...] = jnp.zeros(out_ref.shape, jnp.float32)

    half = LANE // 2
    lane = lax.broadcasted_iota(jnp.int32, (total, LANE), 1)
    inside = lax.broadcasted_iota(jnp.int32, (SUB, LANE), 1) % half // (half // SUB)
    own = jnp.where(inside == lax.broadcasted_iota(jnp.int32, (SUB, LANE), 0), 1.0, 0.0)

    def columns(k, carry):
        x = queries[:, pl.ds(pl.multiple_of(k * LANE, LANE), LANE)]
        swapped = pltpu.roll(x, half, axis=1)
        products = []
        for side in range(2):
            wide = jnp.where((lane < half) == (side == 0), x, swapped)
            high = wide.astype(jnp.bfloat16).astype(jnp.float32)
            spread[0] = high
            spread[1] = wide - high
            terms = []
            for term in range(2):
                lines = [
                    spread[term, pl.ds(q, SUB, stride=0), :] * own for q in range(total)
                ]
                terms.append(jnp.concatenate(lines, axis=0).astype(jnp.bfloat16))
            c = codebook_ref[pl.ds(pl.multiple_of(k * LANE + side * half, half), half), :]
            c_high = c.astype(jnp.bfloat16)
            c_low = (c - c_high.astype(jnp.float32)).astype(jnp.bfloat16)
            weights = jnp.concatenate([c_high, c_low, c_high, c_low], axis=0)
            product = jnp.dot(
                jnp.concatenate(terms, axis=1), weights, preferred_element_type=jnp.float32
            )
            products.append(product.reshape(total, SUB, centres))
        table[:, k] = jnp.concatenate(products, axis=1).astype(jnp.bfloat16)
        return carry

    lax.fori_loop(0, blocks, columns, 0)
    for n in range(lists):
        codes[n] = wide_codes[n].astype(jnp.int16)
    send.wait()
    halves = entries // LANE
    width = lists_s.shape[1]

    def emit(n, chosen, sums):
        for u in range(unroll):
            line = [
                jnp.sum(s, axis=0, keepdims=True) for s in sums[u * halves : (u + 1) * halves]
            ]
            out_ref[n, pl.ds(chosen[u], 1), :] = jnp.concatenate(line, axis=1)

    def group(n, begin, size, inner):
        chosen = [lists_s[n, begin + u] for u in range(size)]
        sums = [None] * (size * halves)
        for i in range(blocks):
            for h in range(halves):
                code = codes[n, i * rows : (i + 1) * rows, h * LANE : (h + 1) * LANE]
                low = jnp.bitwise_and(code, jnp.int16(LANE - 1))
                for u in range(size):
                    value = pick(table[chosen[u], i, :, 0:LANE], low)
                    for part in range(1, centres // LANE):
                        other = pick(table[chosen[u], i, :, part * LANE : (part + 1) * LANE], low)
                        value = jnp.where(code >= jnp.int16(part * LANE), other, value)
                    value = value.astype(jnp.float32)
                    value = value[:SUB] + value[SUB:]
                    at = u * halves + h
                    sums[at] = value if i == 0 else sums[at] + value
            if i == 1:
                emit(*inner)
        chosen += chosen[-1:] * (unroll - size)
        sums += sums[-halves:] * (unroll - size)
        return n, tuple(chosen), tuple(sums)

    short = unroll // 2

    def one_list(n, carry):
        count = lists_s[n, width - 1]
        steps = (count + unroll - short - 1) // unroll
        carry = lax.fori_loop(
            0, steps, lambda step, inner: group(n, step * unroll, unroll, inner), carry
        )
        left = (count - steps * unroll > 0).astype(jnp.int32)
        return lax.fori_loop(
            0, left, lambda step, inner: group(n, steps * unroll, short, inner), carry
        )

    first = (
        jnp.int32(0),
        (jnp.int32(0),) * unroll,
        (jnp.zeros((SUB, LANE), jnp.float32),) * (unroll * halves),
    )
    emit(*lax.fori_loop(0, lists, one_list, first))


def whole(memory=pltpu.VMEM):
    return pl.BlockSpec(memory_space=memory)


def per_device(queries, codebook, pq_codes, probes, vectors, cand_owner, cand_row):
    shards = lax.axis_size("shard")
    owners = lax.axis_size("group") * shards
    q_dev, width = queries.shape
    cands = cand_owner.shape[1]
    subs, centres, dims = codebook.shape
    lists, _, entries = pq_codes.shape
    total = q_dev * shards
    capacity, parts = layout_of(q_dev * cands, owners, width)
    unroll = 8

    ids = pl.pallas_call(
        lambda *refs: ids_kernel(capacity, parts, *refs),
        out_shape=jax.ShapeDtypeStruct((owners, 1, LANE), jnp.int32),
        in_specs=[whole()] * 2,
        out_specs=whole(),
        name="ids",
        cost_estimate=pl.CostEstimate(flops=10**9, bytes_accessed=6 << 20, transcendentals=0),
    )(cand_owner, cand_row)
    list_width = -(-(total + unroll + 1) // LANE) * LANE
    grouping = pl.pallas_call(
        lambda *refs: lists_kernel(lists, owners, *refs),
        out_shape=(
            jax.ShapeDtypeStruct((lists, list_width), jnp.int32),
            jax.ShapeDtypeStruct((q_dev, LANE), jnp.int32),
        ),
        in_specs=[whole()] * 3,
        out_specs=(whole(), whole()),
        name="groups",
        compiler_params=pltpu.CompilerParams(vmem_limit_bytes=4 << 20),
        cost_estimate=pl.CostEstimate(flops=10**9, bytes_accessed=12 << 20, transcendentals=0),
    )
    groups, place = grouping(probes.T, cand_owner, cand_row)
    own, groups = lax.optimization_barrier((queries, groups))
    asked = lax.all_to_all(ids, AXES, split_axis=0, concat_axis=0, tiled=True)

    near = [queries]
    if shards == 8:
        near += [
            lax.ppermute(own, "shard", [(i, i ^ k) for i in range(shards)])
            for k in range(2, shards, 2)
        ]
    else:
        gathered = lax.all_gather(queries, "shard", axis=0, tiled=True)

    paired = capacity * 2 == SUB and parts == 2 and owners % 2 == 0
    piece = width // parts
    kernel, scratch = lambda *refs: rows_kernel(capacity, parts, *refs), []
    if paired:
        kernel = paired_rows_kernel
        scratch = [
            pltpu.VMEM((piece // LANE, owners, SUB, LANE), jnp.bfloat16),
            pltpu.SemaphoreType.DMA((piece // LANE,)),
        ]
    rows = pl.pallas_call(
        kernel,
        out_shape=jax.ShapeDtypeStruct((owners, SUB, piece), jnp.bfloat16),
        in_specs=[whole()] * 2,
        out_specs=whole(pl.ANY) if paired else whole(),
        scratch_shapes=scratch,
        name="rows",
        compiler_params=pltpu.CompilerParams(vmem_limit_bytes=16 << 20),
        cost_estimate=pl.CostEstimate(flops=10**9, bytes_accessed=4 << 20, transcendentals=0),
    )(asked, vectors)
    returned = lax.all_to_all(rows, AXES, split_axis=0, concat_axis=0, tiled=True)
    pieces, chunks = [], []
    if shards == 8:
        joined = pl.pallas_call(
            join_kernel,
            out_shape=jax.ShapeDtypeStruct((len(near) * q_dev, width), jnp.float32),
            in_specs=[whole()] * len(near),
            out_specs=whole(),
            name="join",
            compiler_params=pltpu.CompilerParams(vmem_limit_bytes=4 << 20),
            cost_estimate=pl.CostEstimate(flops=10**9, bytes_accessed=16 << 20, transcendentals=0),
        )(*near)
        other = lax.ppermute(joined, "shard", [(i, i ^ 1) for i in range(shards)])
        for side, chunk in enumerate((joined, other)):
            for n in range(len(near)):
                chunks.append(chunk)
                pieces.append((2 * n ^ side, n * q_dev, q_dev))
    else:
        pieces.append((None, 0, total))
        chunks.append(gathered)

    pq = pl.pallas_call(
        lambda *refs: pq_kernel(q_dev, pieces, unroll, *refs),
        out_shape=jax.ShapeDtypeStruct((lists, total, entries), jnp.float32),
        in_specs=[whole(pl.ANY)] + [whole()] * 2 + [whole()] * len(chunks),
        out_specs=whole(),
        scratch_shapes=[
            pltpu.VMEM((total, width), jnp.float32),
            pltpu.VMEM((2, total, LANE), jnp.float32),
            pltpu.VMEM((total, subs // SUB // 2, 2 * SUB, centres), jnp.bfloat16),
            pltpu.VMEM((lists, subs, entries), jnp.int16),
            pltpu.SMEM((lists, list_width), jnp.int32),
            pltpu.SemaphoreType.DMA((3,)),
        ],
        name="pq",
        compiler_params=pltpu.CompilerParams(
            vmem_limit_bytes=14300000
        ),
        cost_estimate=pl.CostEstimate(
            flops=10**10, bytes_accessed=30 << 20, transcendentals=0
        ),
    )(
        groups,
        codebook.transpose(0, 2, 1).reshape(subs * dims, centres),
        pq_codes,
        *chunks,
    )

    rerank = pl.pallas_call(
        lambda *refs: final_kernel(capacity, parts, *refs),
        out_shape=jax.ShapeDtypeStruct((q_dev, cands), jnp.float32),
        in_specs=[whole()] * 3,
        out_specs=whole(),
        name="final",
        compiler_params=pltpu.CompilerParams(vmem_limit_bytes=8 << 20),
    )(place, queries, returned)
    return pq.transpose(0, 2, 1), rerank


def solution(mesh):
    in_specs = (
        P(AXES, None),
        P(),
        P(AXES, None, None),
        P("group", None),
        P(AXES, None),
        P(AXES, None),
        P(AXES, None),
    )
    out_specs = (P(AXES, None, None), P(AXES, None))
    return jax.shard_map(
        per_device, mesh=mesh, in_specs=in_specs, out_specs=out_specs, check_vma=False
    )
```
